768 devices in a mesh: grp: 4 (over x_hi, core), row: 8 (over y), col: 24 (over z, x_lo).
Axes of the slice: x: 4 (x_hi: 2, x_lo: 2; x = x_hi * 2 + x_lo), y: 8, z: 12, core: 2. Of those that a mesh axis runs over, the one named last changes fastest.
Arguments:
- velocity: float32 [3, 24, 1024, 1024], P(None, 'col', ('grp', 'row')), may hold values from -8 to 8
- profile: int32 [24], P('col'), may hold values from 0 to 1
- x_filters: bfloat16 [2, 1024, 1024], replicated, may hold values from 0 to 1
- z_filter: bfloat16 [1024, 1024], replicated, may hold values from 0 to 1
Outputs:
- stress: float32 [6, 24, 1024, 1024], P(None, 'col', ('grp', 'row'))
The draws below stay inside these ranges and needn't reach their ends.
All inputs are finite; a program needn't handle non-finite values.
Results may differ from the reference program's by a relative error of at most 0.0031.
Values may be sent and summed in bfloat16 or wider, within the bound.
A program may use at most 32 MiB of HBM per device.

```python
import math
import jax
import jax.numpy as jnp
from jax import lax

NX = 1024
NZ = 1024
PROFILES = 2
NY = 24


def filter_stack(key, extent_cells, stack_count):
    width_key, jitter_key = jax.random.split(key)
    narrow = 8.0
    widest = 0.5 * extent_cells
    widths = jnp.exp(jax.random.uniform(width_key, (stack_count, extent_cells, 1), jnp.float32, math.log(narrow), math.log(widest)))
    position = jnp.arange(extent_cells, dtype=jnp.float32)
    distance = jnp.abs(position[:, None] - position[None, :])
    distance = jnp.minimum(distance, extent_cells - distance)
    kernel = jnp.exp(-0.5 * (distance / widths) ** 2) / (2.5066283 * widths)
    jitter = 0.3 * jnp.clip(jax.random.normal(jitter_key, (stack_count, extent_cells, extent_cells), jnp.float32), -1.5, 1.5)
    return 0.5 * jnp.eye(extent_cells, dtype=jnp.float32) + 0.5 * kernel * (1.0 + jitter)


def draw_x_filters(key, part):
    return filter_stack(jax.random.fold_in(key, 3), NX, PROFILES).astype(jnp.bfloat16)


def draw_z_filter(key, part):
    return filter_stack(jax.random.fold_in(key, 7), NZ, 1)[0].astype(jnp.bfloat16)


def plant(drawn, rng, least, largest):
    shape = drawn.shape
    place = [jax.random.randint(jax.random.fold_in(rng, axis), (), 0, shape[axis]) for axis in range(len(shape))]
    drawn = drawn.at[tuple(place)].set(least)
    longest = shape.index(max(shape))
    place[longest] = (place[longest] + 1) % shape[longest]
    return drawn.at[tuple(place)].set(largest)


def shard_levels(own_key, shape, pieces, least, top_value):
    factor_of, own = 1.0, jax.random.fold_in(own_key, 6)
    for axis_at, parts in pieces:
        steps = jnp.exp(jax.random.uniform(jax.random.fold_in(own, axis_at), (parts,), jnp.float32, least / len(pieces), top_value / len(pieces)))
        factor_of = factor_of * jnp.repeat(steps, shape[axis_at] // parts).reshape([-1 if axis == axis_at else 1 for axis in range(len(shape))])
    return factor_of


def noise(own_key, dims, deviation, reach, cuts=(), kind=jnp.bfloat16):
    factor_of = shard_levels(own_key, dims, cuts, -0.22, 0.18) if cuts else 1.0
    values = jax.random.normal(own_key, dims, jnp.float32) * deviation * factor_of
    return jnp.minimum(jnp.maximum(values, -reach), reach).astype(kind)


def setup_inputs(seed: int = 0) -> dict:
    key_list = jax.random.split(jax.random.key(seed), 5)
    velocity = noise(key_list[0], (3, NY, NZ, NX), 2.0, 8.0, ((1, 24), (2, 32)), jnp.float32)
    profile = plant(jax.random.randint(key_list[1], (NY,), 0, PROFILES), jax.random.fold_in(key_list[1], 1), 0, PROFILES - 1).astype(jnp.int32)
    x_filters = draw_x_filters(jax.random.fold_in(key_list[4], 71), 0)
    z_filter = draw_z_filter(jax.random.fold_in(key_list[4], 71), 0)
    return dict(velocity=velocity, profile=profile, x_filters=x_filters, z_filter=z_filter)


STEP_SIZE = 0.25
VISCOSITY = 0.8
PRODUCT_PAIRS = ((0, 0), (0, 1), (0, 2), (1, 1), (1, 2), (2, 2))


def row_rate(window):
    center = window[:, 1]
    y_next = window[:, 2]
    y_prev = window[:, 0]
    z_next = jnp.roll(center, -1, axis=1)
    z_prev = jnp.roll(center, 1, axis=1)
    x_next = jnp.roll(center, -1, axis=2)
    x_prev = jnp.roll(center, 1, axis=2)
    advect = center[0] * (0.5 * (x_next - x_prev)) + center[1] * (0.5 * (y_next - y_prev)) + center[2] * (0.5 * (z_next - z_prev))
    laplace = x_next + x_prev + y_next + y_prev + z_next + z_prev - 6.0 * center
    return VISCOSITY * laplace - advect


def velocity_rate(values):
    padded = jnp.pad(values, ((0, 0), (1, 1), (0, 0), (0, 0)))

    def one_row(row_number):
        return row_rate(lax.dynamic_slice_in_dim(padded, row_number, 3, 1))

    stacked = lax.map(one_row, jnp.arange(values.shape[1], dtype=jnp.int32))
    return jnp.transpose(stacked, (1, 0, 2, 3))


def reference(velocity, profile, x_filters, z_filter):
    section_one = velocity + STEP_SIZE * velocity_rate(velocity)
    section_two = 0.75 * velocity + 0.25 * (section_one + STEP_SIZE * velocity_rate(section_one))
    advanced = velocity / 3.0 + (2.0 / 3.0) * (section_two + STEP_SIZE * velocity_rate(section_two))

    def analyse(row_number):
        planes = lax.dynamic_index_in_dim(advanced, row_number, 1, keepdims=False)
        components = [planes[0], planes[1], planes[2]] + [planes[left_comp] * planes[right_comp] for left_comp, right_comp in PRODUCT_PAIRS]
        fields = jnp.stack(components).astype(jnp.bfloat16)
        matrix = lax.dynamic_index_in_dim(x_filters, profile[row_number], 0, keepdims=False)
        x_pass = jnp.einsum("ox,fzx->foz", matrix.astype(jnp.float32), fields.astype(jnp.float32)).astype(jnp.bfloat16)
        z_pass = jnp.einsum("fos,rs->for", x_pass.astype(jnp.float32), z_filter.astype(jnp.float32))
        return jnp.stack([z_pass[3 + number] - z_pass[left_comp] * z_pass[right_comp] for number, (left_comp, right_comp) in enumerate(PRODUCT_PAIRS)])

    stress = lax.map(analyse, jnp.arange(velocity.shape[1], dtype=jnp.int32))
    return jnp.transpose(stress, (1, 0, 2, 3))
```

```python
import functools

import jax
import jax.numpy as jnp
from jax import lax
from jax.experimental import pallas as pl
from jax.experimental.pallas import tpu as pltpu
from jax.sharding import PartitionSpec as P

F32 = jnp.float32
BF16 = jnp.bfloat16
MESH = pl.DeviceIdType.MESH
PRODUCT_PAIRS = ((0, 0), (0, 1), (0, 2), (1, 1), (1, 2), (2, 2))
FIELD_FACTORS = ((0,), (1,), (2,)) + PRODUCT_PAIRS

DEPTH = 3
HALF = 16
WIDE = HALF + 2 * DEPTH
ROWS = 2 + 2 * DEPTH
CELLS = ROWS * WIDE
DISTANCE = (3, 2, 1, 0, 0, 1, 2, 3)
CODE_MAX = 32767.0
BOUND = 8.0


def encode(value):
    root = jnp.sqrt(jnp.sqrt(jnp.abs(value) * (1.0 / BOUND)))
    code = (root * CODE_MAX + 0.5).astype(jnp.int32)
    return jnp.where(value < 0.0, -code, code).astype(jnp.int16)


def decode(code):
    root = code.astype(jnp.int32).astype(F32) * (1.0 / CODE_MAX)
    return (root * jnp.abs(root)) * (root * root * BOUND)


def kernel(
    sizes,
    profile_ref, velocity_ref, x_hbm, z_hbm, out_ref,
    spread, coded, gathered, wide, first, second, advanced, fields,
    x_mat, z_mat, send_main, send_last, recv_main, recv_last, z_pass,
    weight_sem, gather_send, gather_recv, local_sem, pass_send, pass_recv,
):
    n_grp, n_row, n_col = sizes
    n_blk, n_pln = n_grp * n_row, n_col // 2
    grp, row, col = lax.axis_index("grp"), lax.axis_index("row"), lax.axis_index("col")
    blk = grp * n_row + row
    pln, half = col // 2, col % 2
    other = 1 - half

    def device(block, plane, side):
        block = lax.rem(block + n_blk, n_blk)
        plane = lax.rem(plane + n_pln, n_pln)
        return (block // n_row, lax.rem(block, n_row), plane * 2 + side)

    barrier = pltpu.get_barrier_semaphore()

    def say(target):
        pl.semaphore_signal(barrier, inc=1, device_id=target, device_id_type=MESH)

    beside = blk - 1 + 2 * half
    for step in (-1, 1):
        for side in (0, 1):
            say(device(blk, pln + step, side))
            say(device(beside, pln + step, side))
    say(device(blk, pln - 2, 1))
    say(device(blk, pln + 2, 0))
    say(device(blk, pln, other))

    def say_block(step, carry):
        say(device(blk + step, pln, 0))
        say(device(blk + step, pln, 1))
        return carry

    lax.fori_loop(1, n_blk, say_block, 0)
    partners = 2 * n_blk - 1 + 10

    x_copy = pltpu.make_async_copy(x_hbm, x_mat, weight_sem.at[0])
    z_copy = pltpu.make_async_copy(z_hbm, z_mat, weight_sem.at[1])
    x_copy.start()
    z_copy.start()

    for comp in range(3):
        for group in range(4):
            for chunk in range(8):
                spread[comp, pl.ds(group * 64 + chunk, 8, stride=8), :] = velocity_ref[
                    comp, 0, group * 8:(group + 1) * 8, chunk * 128:(chunk + 1) * 128
                ]

    def encode_cell(cell, carry):
        start = pl.multiple_of(cell * 8, 8)
        for comp in range(3):
            coded[cell, comp] = encode(spread[comp, pl.ds(start, 8), :])
        return carry

    lax.fori_loop(0, 2 * HALF, encode_cell, 0)
    own_profile = jnp.full((8, 128), profile_ref[0], jnp.int32).astype(F32)
    for comp in range(3):
        coded[2 * HALF, comp] = own_profile.astype(jnp.int32).astype(jnp.int16)

    pl.semaphore_wait(barrier, partners)

    def give(source, count, place, target):
        pltpu.make_async_remote_copy(
            src_ref=coded.at[pl.ds(source, count)],
            dst_ref=gathered.at[pl.ds(place, count)],
            send_sem=gather_send, recv_sem=gather_recv,
            device_id=target, device_id_type=MESH,
        ).start()

    far_step = 4 * half - 2
    far_row = 7 * other
    for side in (0, 1):
        give(HALF * side, HALF, far_row * WIDE + DEPTH, device(blk, pln + far_step, side))
    for step in (-1, 1):
        place = (DEPTH + half - 2 * step) * WIDE
        give(0, HALF + 2, place + DEPTH, device(blk, pln + step, 0))
        give(HALF - 2, HALF + 2, place + DEPTH - 2, device(blk, pln + step, 1))
        give(2 * HALF - 2, 2, place + DEPTH - 2, device(blk + 1, pln + step, 0))
        give(0, 2, place + DEPTH + HALF, device(blk - 1, pln + step, 1))
    place = (DEPTH + half) * WIDE
    give(
        (HALF - DEPTH) * other, HALF + DEPTH, place + DEPTH - DEPTH * other,
        device(blk, pln, other),
    )
    give(2 * HALF - DEPTH, DEPTH, place, device(blk + 1, pln, 0))
    give(0, DEPTH, place + DEPTH + HALF, device(blk - 1, pln, 1))
    give(2 * HALF, 1, CELLS, device(blk, pln, other))
    own = pltpu.make_async_copy(
        coded.at[pl.ds((HALF - DEPTH) * half, HALF + DEPTH)],
        gathered.at[pl.ds(place + DEPTH - DEPTH * half, HALF + DEPTH)],
        local_sem.at[0],
    )
    own.start()
    own.wait()
    moved = 138
    pltpu.make_async_copy(
        gathered.at[pl.ds(0, moved)], gathered.at[pl.ds(0, moved)], gather_recv
    ).wait()

    inside = [
        jnp.where(
            (2 * pln - DEPTH + place_row >= 0) & (2 * pln - DEPTH + place_row < n_col), 1.0, 0.0
        ).astype(F32)
        for place_row in range(ROWS)
    ]

    for place_row in range(ROWS):
        reach = DEPTH - DISTANCE[place_row]

        def decode_cell(cell, carry, place_row=place_row):
            for comp in range(3):
                wide[place_row * WIDE + cell, comp] = (
                    decode(gathered[place_row * WIDE + cell, comp]) * inside[place_row]
                )
            return carry

        lax.fori_loop(DEPTH - reach, DEPTH + HALF + reach, decode_cell, 0)

    lane = lax.broadcasted_iota(jnp.int32, (8, 128), 1)
    last_lane, first_lane = lane == 127, lane == 0

    def stage(source, keep, old, store):
        weight, advect = 0.2 * keep, 0.125 * keep

        def cell_of(place_row, cell):
            here = place_row * WIDE + cell
            center = [source[here, comp] for comp in range(3)]
            pairs = []
            for comp in range(3):
                scaled = center[comp] * advect
                pairs.append((weight - scaled, weight + scaled))
            for comp in range(3):
                value = center[comp]
                ahead = pltpu.roll(value, 127, 1)
                ahead = jnp.where(last_lane, pltpu.roll(ahead, 7, 0), ahead)
                behind = pltpu.roll(value, 1, 1)
                behind = jnp.where(first_lane, pltpu.roll(behind, 1, 0), behind)
                total = (pairs[0][0] * ahead + pairs[0][1] * behind) + (
                    pairs[1][0] * source[here + WIDE, comp]
                    + pairs[1][1] * source[here - WIDE, comp]
                )
                total = total + (
                    pairs[2][0] * source[here + 1, comp] + pairs[2][1] * source[here - 1, comp]
                )
                total = total - weight * value
                if old:
                    total = total + old * wide[here, comp]
                store(place_row, cell, comp, total)

        return cell_of

    def sweep(number, cell_of):
        for place_row in range(ROWS):
            reach = DEPTH - number - DISTANCE[place_row]
            if reach < 0:
                continue

            def two(step, carry, place_row=place_row, low=DEPTH - reach):
                cell_of(place_row, low + 2 * step)
                cell_of(place_row, low + 2 * step + 1)
                return carry

            lax.fori_loop(0, (HALF + 2 * reach) // 2, two, 0)

    def into(target):
        def store(place_row, cell, comp, value):
            if DISTANCE[place_row]:
                value = value * inside[place_row]
            target[place_row * WIDE + cell, comp] = value

        return store

    def into_advanced(place_row, cell, comp, value):
        start = pl.multiple_of(((place_row - DEPTH) * HALF + cell - DEPTH) * 8, 8)
        advanced[comp, pl.ds(start, 8), :] = value

    sweep(1, stage(wide, 1.0, None, into(first)))
    sweep(2, stage(first, 0.25, 0.75, into(second)))
    sweep(3, stage(second, 2.0 / 3.0, 1.0 / 3.0, into_advanced))

    pair_profile = gathered[CELLS, 0].astype(jnp.int32).astype(F32)
    even = jnp.where(half == 0, own_profile, pair_profile)
    odd = jnp.where(half == 0, pair_profile, own_profile)
    one = jnp.concatenate([even, even, odd, odd], axis=0)
    zero = 1.0 - one
    for chunk in range(8):
        comps = [advanced[comp, pl.ds(chunk, 2 * HALF, stride=8), :] for comp in range(3)]
        for number, factors in enumerate(FIELD_FACTORS):
            field = functools.reduce(lambda a, b: a * b, [comps[f] for f in factors])
            rows = slice(number * 2 * HALF, (number + 1) * 2 * HALF)
            fields[rows, chunk * 128:(chunk + 1) * 128] = (field * zero).astype(BF16)
            fields[rows, 1024 + chunk * 128:1024 + (chunk + 1) * 128] = (field * one).astype(BF16)

    x_copy.wait()
    wide_lane = lax.broadcasted_iota(jnp.int32, (2 * HALF, 128), 1)
    quarter = wide_lane // 32
    small_quarter = lane // 32

    def outputs(step, carry):
        dest_grp = lax.rem(grp + 1 + step, n_grp)
        start = pl.multiple_of(dest_grp * n_row * 32, 256)
        contract = (((1,), (1,)), ((), ()))
        passed = lax.dot_general(
            fields[:, 0:1024], x_mat[0, pl.ds(start, 256), :], contract,
            preferred_element_type=F32,
        ) + lax.dot_general(
            fields[:, 1024:2048], x_mat[1, pl.ds(start, 256), :], contract,
            preferred_element_type=F32,
        )
        for tile in range(2):
            lanes = slice(tile * 128, (tile + 1) * 128)
            for part in range(2):
                turned = []
                for k in range(4):
                    piece = passed[(part * 4 + k) * 32:(part * 4 + k + 1) * 32, lanes]
                    turned.append(pltpu.roll(piece, 32 * k, 1) if k else piece)
                for place in range(4):
                    mixed = turned[3]
                    for k in range(3):
                        mixed = jnp.where(quarter == (place + k) % 4, turned[k], mixed)
                    mixed = mixed.astype(BF16)
                    dest = dest_grp * n_row + tile * 4 + place
                    send_main[part, dest] = mixed[0:HALF]
                    send_main[part, n_blk + dest] = mixed[HALF:2 * HALF]
            for line in range(2):
                low = passed[256 + line * HALF:256 + line * HALF + 8, lanes]
                high = pltpu.roll(passed[256 + line * HALF + 8:256 + (line + 1) * HALF, lanes], 32, 1)
                for place in range(4):
                    dest = dest_grp * n_row + tile * 4 + place
                    send_last[line * n_blk + dest] = jnp.where(
                        small_quarter == place, low, high
                    ).astype(BF16)
        spot = 2 * blk + half
        for off in (4, 3, 5, 2, 6, 1, 7, 0):
            dest_row = lax.rem(row + off, n_row)
            dest = dest_grp * n_row + dest_row
            for line in range(2):
                target = (dest_grp, dest_row, 2 * pln + line)

                def send(line=line, target=target, dest=dest):
                    for part in range(2):
                        pltpu.make_async_remote_copy(
                            src_ref=send_main.at[part, line * n_blk + dest],
                            dst_ref=recv_main.at[part, spot],
                            send_sem=pass_send.at[part], recv_sem=pass_recv.at[part],
                            device_id=target, device_id_type=MESH,
                        ).start()
                    pltpu.make_async_remote_copy(
                        src_ref=send_last.at[line * n_blk + dest],
                        dst_ref=recv_last.at[spot],
                        send_sem=pass_send.at[2], recv_sem=pass_recv.at[2],
                        device_id=target, device_id_type=MESH,
                    ).start()

                if off:
                    send()
                else:
                    pl.when((dest != blk) | (half != line))(send)
        return carry

    lax.fori_loop(0, n_grp, outputs, 0)
    spot = 2 * blk + half
    mine = half * n_blk + blk
    stays = [
        pltpu.make_async_copy(send_main.at[part, mine], recv_main.at[part, spot], local_sem.at[1 + part])
        for part in range(2)
    ]
    stays.append(pltpu.make_async_copy(send_last.at[mine], recv_last.at[spot], local_sem.at[3]))
    for stay in stays:
        stay.start()
    z_copy.wait()
    for stay in stays:
        stay.wait()

    contract = (((0,), (1,)), ((), ()))
    many = 2 * n_blk - 1
    for part in range(2):
        pltpu.make_async_copy(
            recv_main.at[part, pl.ds(0, many)], recv_main.at[part, pl.ds(0, many)], pass_recv.at[part]
        ).wait()
        lines = recv_main[part].reshape(2 * n_blk * HALF, 128)
        z_pass[part * 128:(part + 1) * 128, :] = lax.dot_general(
            lines, z_mat[...], contract, preferred_element_type=F32
        )
    pltpu.make_async_copy(
        recv_last.at[pl.ds(0, many)], recv_last.at[pl.ds(0, many)], pass_recv.at[2]
    ).wait()
    low = recv_last[...].astype(F32)
    high = pltpu.roll(low.reshape(2 * n_blk * 8, 128), 96, 1).reshape(2 * n_blk, 8, 128)
    lines = jnp.concatenate([low, high], axis=1).reshape(2 * n_blk * HALF, 128).astype(BF16)
    z_pass[256:384, :] = lax.dot_general(lines, z_mat[...], contract, preferred_element_type=F32)

    turn = lax.rem(row, 4)

    def filtered(number):
        part, k = number // 4, number % 4
        start = part * 128 + lax.rem(turn + k, 4) * 32
        return z_pass[pl.ds(pl.multiple_of(start, 32), 32), :]

    linear = [filtered(number) for number in range(3)]
    for number, (left, right) in enumerate(PRODUCT_PAIRS):
        out_ref[number, 0] = filtered(3 + number) - linear[left] * linear[right]

    pltpu.make_async_copy(
        gathered.at[pl.ds(0, moved)], gathered.at[pl.ds(0, moved)], gather_send
    ).wait()
    for part in range(2):
        pltpu.make_async_copy(
            send_main.at[part, pl.ds(0, many)], send_main.at[part, pl.ds(0, many)], pass_send.at[part]
        ).wait()
    pltpu.make_async_copy(
        send_last.at[pl.ds(0, many)], send_last.at[pl.ds(0, many)], pass_send.at[2]
    ).wait()


def solution(mesh):
    sizes = (mesh.shape["grp"], mesh.shape["row"], mesh.shape["col"])
    n_blk = sizes[0] * sizes[1]
    tile = (8, 128)

    def body(velocity, profile, x_filters, z_filter):
        vmem = pl.BlockSpec(memory_space=pltpu.VMEM)
        return pl.pallas_call(
            functools.partial(kernel, sizes),
            out_shape=jax.ShapeDtypeStruct((6, 1, 32, 1024), F32),
            in_specs=[
                pl.BlockSpec(memory_space=pltpu.SMEM),
                vmem,
                pl.BlockSpec(memory_space=pl.ANY),
                pl.BlockSpec(memory_space=pl.ANY),
            ],
            out_specs=vmem,
            scratch_shapes=[
                pltpu.VMEM((3, 256, 128), F32),
                pltpu.VMEM((2 * HALF + 1, 3) + tile, jnp.int16),
                pltpu.VMEM((CELLS + 1, 3) + tile, jnp.int16),
                pltpu.VMEM((CELLS, 3) + tile, F32),
                pltpu.VMEM((CELLS, 3) + tile, F32),
                pltpu.VMEM((CELLS, 3) + tile, F32),
                pltpu.VMEM((3, 256, 128), F32),
                pltpu.VMEM((9 * 2 * HALF, 2048), BF16),
                pltpu.VMEM((2, 1024, 1024), BF16),
                pltpu.VMEM((1024, 1024), BF16),
                pltpu.VMEM((2, 2 * n_blk, HALF, 128), BF16),
                pltpu.VMEM((2 * n_blk, 8, 128), BF16),
                pltpu.VMEM((2, 2 * n_blk, HALF, 128), BF16),
                pltpu.VMEM((2 * n_blk, 8, 128), BF16),
                pltpu.VMEM((384, 1024), F32),
                pltpu.SemaphoreType.DMA((2,)),
                pltpu.SemaphoreType.DMA,
                pltpu.SemaphoreType.DMA,
                pltpu.SemaphoreType.DMA((4,)),
                pltpu.SemaphoreType.DMA((3,)),
                pltpu.SemaphoreType.DMA((3,)),
            ],
            compiler_params=pltpu.CompilerParams(
                collective_id=0, has_side_effects=True, vmem_limit_bytes=60000 * 1024
            ),
            name="subgrid",
        )(profile, velocity, x_filters, z_filter)

    placed = (P(None, "col", ("grp", "row"), None), P("col"), P(), P())
    return jax.shard_map(
        body,
        mesh=mesh,
        in_specs=placed,
        out_specs=P(None, "col", ("grp", "row"), None),
        check_vma=False,
    )
```

```python
import functools

import jax
import jax.numpy as jnp
from jax import lax
from jax.experimental import pallas as pl
from jax.experimental.pallas import tpu as pltpu
from jax.sharding import PartitionSpec as P

F32 = jnp.float32
BF16 = jnp.bfloat16
MESH = pl.DeviceIdType.MESH
PRODUCT_PAIRS = ((0, 0), (0, 1), (0, 2), (1, 1), (1, 2), (2, 2))
FIELD_FACTORS = ((0,), (1,), (2,)) + PRODUCT_PAIRS

DEPTH = 3
HALF = 16
PART = 8
WIDE = HALF + 2 * DEPTH
ROWS = 2 + 2 * DEPTH
CELLS = ROWS * WIDE
CODE_MAX = 32767.0
BOUND = 8.0


def encode(value):
    root = jnp.sqrt(jnp.sqrt(jnp.abs(value) * (1.0 / BOUND)))
    code = (root * CODE_MAX + 0.5).astype(jnp.int32)
    return jnp.where(value < 0.0, -code, code).astype(jnp.int16)


def decode(code):
    root = code.astype(jnp.int32).astype(F32) * (1.0 / CODE_MAX)
    return (root * jnp.abs(root)) * (root * root * BOUND)


def kernel(
    sizes,
    profile_ref, velocity_ref, x_hbm, z_hbm, direct_ref, product_ref,
    spread, coded, gathered, wide, first, second, advanced, fields, last_low,
    x_mat, z_mat, send_first, send_second, recv_first, recv_second, z_pass,
    weight_sem, gather_send, gather_recv, profile_sem, local_sem, pass_send, pass_recv,
):
    n_grp, n_row, n_col = sizes
    n_blk, n_pln = n_grp * n_row, n_col // 2
    grp, row, col = lax.axis_index("grp"), lax.axis_index("row"), lax.axis_index("col")
    blk = grp * n_row + row
    pln, half = col // 2, col % 2
    other = 1 - half
    toward = 2 * half - 1

    def there(plane):
        return (plane >= 0) & (plane < n_pln)

    def device(block, plane, side):
        block = lax.rem(block + n_blk, n_blk)
        return (block // n_row, lax.rem(block, n_row), plane * 2 + side)

    barrier = pltpu.get_barrier_semaphore()

    def say(target):
        pl.semaphore_signal(barrier, inc=1, device_id=target, device_id_type=MESH)

    beside = blk + toward
    for step in (-1, 1):
        @pl.when(there(pln + step))
        def _(step=step):
            for side in (0, 1):
                say(device(blk, pln + step, side))
                say(device(beside, pln + step, side))

    @pl.when(there(pln - 2))
    def _():
        say(device(blk, pln - 2, 1))

    @pl.when(there(pln + 2))
    def _():
        say(device(blk, pln + 2, 0))

    say(device(blk, pln, other))

    def say_block(step, carry):
        say(device(blk + step, pln, 0))
        say(device(blk + step, pln, 1))
        return carry

    lax.fori_loop(1, n_blk, say_block, 0)

    x_copy = pltpu.make_async_copy(x_hbm, x_mat, weight_sem.at[0])
    z_copy = pltpu.make_async_copy(z_hbm, z_mat, weight_sem.at[1])
    x_copy.start()
    z_copy.start()

    for group in range(4):
        for comp in range(3):
            for chunk in range(8):
                spread[comp, pl.ds(group * 64 + chunk, 8, stride=8), :] = velocity_ref[
                    comp, 0, group * 8:(group + 1) * 8, chunk * 128:(chunk + 1) * 128
                ]

    def encode_cells(step, carry):
        for cell in range(4):
            start = pl.multiple_of((step * 4 + cell) * 8, 8)
            for comp in range(3):
                coded[step * 4 + cell, comp] = encode(spread[comp, pl.ds(start, 8), :])
        return carry

    lax.fori_loop(0, 2 * HALF // 4, encode_cells, 0)
    own_profile = jnp.full((8, 128), profile_ref[0], jnp.int32)
    for comp in range(3):
        coded[2 * HALF, comp] = own_profile.astype(jnp.int16)

    partners = 2 * n_blk - 1
    for step, count in ((toward, 4), (-toward, 4), (2 * toward, 2)):
        partners = partners + jnp.where(there(pln + step), count, 0)
    pl.semaphore_wait(barrier, partners)

    def give(source, count, cell, part, line, kind, target):
        pltpu.make_async_remote_copy(
            src_ref=coded.at[pl.ds(source, count)],
            dst_ref=gathered.at[pl.ds(line * WIDE + cell, count)],
            send_sem=gather_send.at[kind], recv_sem=gather_recv.at[part, line],
            device_id=target, device_id_type=MESH,
        ).start()

    pltpu.make_async_remote_copy(
        src_ref=coded.at[pl.ds(2 * HALF, 1)], dst_ref=gathered.at[pl.ds(CELLS, 1)],
        send_sem=gather_send.at[4], recv_sem=profile_sem,
        device_id=device(blk, pln, other), device_id_type=MESH,
    ).start()

    own_line = DEPTH + half
    lines = (own_line, 5 - 3 * half, 1 + 5 * half, 7 - 7 * half)
    steps = (0, toward, -toward, 2 * toward)
    for part in range(2):
        for d in range(4):
            def main(side, d=d, part=part):
                target = device(blk, pln + steps[d], side)
                if part == 0 and side == 0:
                    give(0, 11 - d, DEPTH, part, lines[d], d, target)
                elif part == 0:
                    give(13 + d, 14 - 2 * d, d, part, lines[d], d, target)
                elif side == 0:
                    give(11 - d, PART, 14 - d, part, lines[d], d, target)
                else:
                    give(27 - d, 5 + d, 14 - d, part, lines[d], d, target)

            def strip(d=d, part=part):
                if d == 3:
                    return
                if part == 0:
                    give(29 + d, 3 - d, d, part, lines[d], d, device(blk + 1, pln + steps[d], 0))
                else:
                    give(0, 3 - d, DEPTH + HALF, part, lines[d], d, device(blk - 1, pln + steps[d], 1))

            if d == 0:
                for side in (0, 1):
                    pl.when(half != side)(functools.partial(main, side))
                strip()
            else:
                @pl.when(there(pln + steps[d]))
                def _(main=main, strip=strip):
                    main(0)
                    main(1)
                    strip()

    present = [
        (2 * pln - DEPTH + line >= 0) & (2 * pln - DEPTH + line < n_col) for line in range(ROWS)
    ]
    inside = [jnp.where(known, 1.0, 0.0).astype(F32) for known in present]

    for line in (0, 1, 2, 5, 6, 7):
        @pl.when(jnp.logical_not(present[line]))
        def _(line=line):
            def clear(cell, carry):
                for comp in range(3):
                    wide[line * WIDE + cell, comp] = jnp.zeros((8, 128), F32)
                return carry

            lax.fori_loop(0, WIDE, clear, 0)

    def keep(cell, carry):
        start = pl.multiple_of(((HALF - DEPTH) * half + cell) * 8, 8)
        for comp in range(3):
            wide[own_line * WIDE + DEPTH * other + cell, comp] = spread[comp, pl.ds(start, 8), :]
        return carry

    lax.fori_loop(0, HALF + DEPTH, keep, 0)

    def arrive(part, line, low, count):
        pltpu.make_async_copy(
            gathered.at[pl.ds(0, count)], gathered.at[pl.ds(0, count)], gather_recv.at[part, line]
        ).wait()
        per = 2 if count % 2 == 0 else 1

        def some(step, carry):
            for cell in range(per):
                here = line * WIDE + low + step * per + cell
                for comp in range(3):
                    wide[here, comp] = decode(gathered[here, comp])
            return carry

        lax.fori_loop(0, count // per, some, 0)

    lane = lax.broadcasted_iota(jnp.int32, (8, 128), 1)
    last_lane, first_lane = lane == 127, lane == 0

    def advance(source, scale, old, here):
        weight, advect = 0.2 * scale, 0.125 * scale
        center = [source[here, comp] for comp in range(3)]
        pairs = []
        for comp in range(3):
            scaled = center[comp] * advect
            pairs.append((weight - scaled, weight + scaled))
        results = []
        for comp in range(3):
            value = center[comp]
            ahead = pltpu.roll(value, 127, 1)
            ahead = jnp.where(last_lane, pltpu.roll(ahead, 7, 0), ahead)
            behind = pltpu.roll(value, 1, 1)
            behind = jnp.where(first_lane, pltpu.roll(behind, 1, 0), behind)
            total = (pairs[0][0] * ahead + pairs[0][1] * behind) + (
                pairs[1][0] * source[here + WIDE, comp] + pairs[1][1] * source[here - WIDE, comp]
            )
            total = total + (
                pairs[2][0] * source[here + 1, comp] + pairs[2][1] * source[here - 1, comp]
            )
            total = total - weight * value
            if old:
                total = total + old * wide[here, comp]
            results.append(total)
        return results

    def sweep(number, part, d):
        source = (wide, first, second)[number - 1]
        scale, old = ((1.0, None), (0.25, 0.75), (2.0 / 3.0, 1.0 / 3.0))[number - 1]
        low, high = ((d + number, 14 - d - number), (14 - d - number, 22 - d - number))[part]

        def two(step, carry):
            done = []
            for line in (DEPTH - d, DEPTH + 1 + d):
                for cell in range(2):
                    place = low + 2 * step + cell
                    done.append((line, place, advance(source, scale, old, line * WIDE + place)))
            for line, place, results in done:
                for comp in range(3):
                    value = results[comp]
                    if number == 3:
                        start = ((part * 2 + line - DEPTH) * PART + place - low) * 8
                        advanced[comp, pl.ds(pl.multiple_of(start, 8), 8), :] = value
                        continue
                    if d:
                        value = value * inside[line]
                    (first, second)[number - 1][line * WIDE + place, comp] = value
            return carry

        lax.fori_loop(0, (high - low) // 2, two, 0)

    wide_lane = lax.broadcasted_iota(jnp.int32, (2 * PART, 128), 1)
    quarter = wide_lane // 32
    small_quarter = lane // 32
    spot = 2 * blk + half

    def pass_part(part, one, zero):
        for chunk in range(8):
            comps = [
                advanced[comp, pl.ds(part * 128 + chunk, 2 * PART, stride=8), :] for comp in range(3)
            ]
            for number, factors in enumerate(FIELD_FACTORS):
                field = functools.reduce(lambda a, b: a * b, [comps[f] for f in factors])
                rows = slice(number * 2 * PART, (number + 1) * 2 * PART)
                fields[rows, chunk * 128:(chunk + 1) * 128] = (field * zero).astype(BF16)
                fields[rows, 1024 + chunk * 128:1024 + (chunk + 1) * 128] = (field * one).astype(BF16)
        send_ref = (send_first, send_second)[part]
        recv_ref = (recv_first, recv_second)[part]

        def outputs(step, carry):
            dest_grp = lax.rem(grp + 1 + step, n_grp)
            start = pl.multiple_of(dest_grp * n_row * 32, 256)
            contract = (((1,), (1,)), ((), ()))
            passed = lax.dot_general(
                fields[:, 0:1024], x_mat[0, pl.ds(start, 256), :], contract,
                preferred_element_type=F32,
            ) + lax.dot_general(
                fields[:, 1024:2048], x_mat[1, pl.ds(start, 256), :], contract,
                preferred_element_type=F32,
            )
            if part == 0:
                last_low[:, pl.ds(start, 256)] = passed[128:144]
            else:
                lows = last_low[:, pl.ds(start, 256)]
            for tile in range(2):
                lanes = slice(tile * 128, (tile + 1) * 128)
                for four in range(2):
                    turned = []
                    for k in range(4):
                        piece = passed[(four * 4 + k) * 16:(four * 4 + k + 1) * 16, lanes]
                        turned.append(pltpu.roll(piece, 32 * k, 1) if k else piece)
                    for place in range(4):
                        mixed = turned[3]
                        for k in range(3):
                            mixed = jnp.where(quarter == (place + k) % 4, turned[k], mixed)
                        dest = dest_grp * n_row + tile * 4 + place
                        send_ref[dest, four] = mixed[0:PART].astype(BF16)
                        send_ref[n_blk + dest, four] = mixed[PART:2 * PART].astype(BF16)
                if part == 1:
                    for line in range(2):
                        rows = slice(line * PART, (line + 1) * PART)
                        high = pltpu.roll(passed[128:144, lanes][rows], 32, 1)
                        low = lows[rows, lanes]
                        for place in range(4):
                            dest = dest_grp * n_row + tile * 4 + place
                            send_ref[line * n_blk + dest, 2] = jnp.where(
                                small_quarter == place, low, high
                            ).astype(BF16)
            for off in (4, 3, 5, 2, 6, 1, 7, 0):
                dest_row = lax.rem(row + off, n_row)
                dest = dest_grp * n_row + dest_row
                for line in range(2):
                    target = (dest_grp, dest_row, 2 * pln + line)

                    def send(line=line, target=target, dest=dest):
                        pltpu.make_async_remote_copy(
                            src_ref=send_ref.at[line * n_blk + dest], dst_ref=recv_ref.at[spot],
                            send_sem=pass_send.at[part], recv_sem=pass_recv.at[part],
                            device_id=target, device_id_type=MESH,
                        ).start()

                    if off:
                        send()
                    else:
                        pl.when((dest != blk) | (half != line))(send)
            return carry

        lax.fori_loop(0, n_grp, outputs, 0)
        stay = pltpu.make_async_copy(
            send_ref.at[half * n_blk + blk], recv_ref.at[spot], local_sem.at[part]
        )
        stay.start()
        return stay

    stays = []
    for part in range(2):
        for d in range(4):
            if d == 0:
                arrive(part, 4 - half, (0, 14)[part], (14, PART)[part])
                pl.when(half == part)(
                    functools.partial(arrive, part, own_line, (0, DEPTH + HALF)[part], DEPTH)
                )
                continue
            for line in (DEPTH - d, DEPTH + 1 + d):
                pl.when(present[line])(
                    functools.partial(arrive, part, line, (d, 14 - d)[part], (14 - 2 * d, PART)[part])
                )
            for number in range(1, d + 1):
                sweep(number, part, d - number)
        if part == 0:
            pltpu.make_async_copy(
                gathered.at[pl.ds(0, 1)], gathered.at[pl.ds(0, 1)], profile_sem
            ).wait()
            pair_profile = gathered[CELLS, 0].astype(jnp.int32)
            even = jnp.where(half == 0, own_profile, pair_profile).astype(F32)
            odd = jnp.where(half == 0, pair_profile, own_profile).astype(F32)
            one = jnp.concatenate([even, odd], axis=0)
            x_copy.wait()
        stays.append(pass_part(part, one, 1.0 - one))
    z_copy.wait()

    contract = (((0,), (1,)), ((), ()))
    many = 2 * n_blk - 1
    for part, ref in ((0, recv_first), (1, recv_second)):
        stays[part].wait()
        pltpu.make_async_copy(
            ref.at[pl.ds(0, many)], ref.at[pl.ds(0, many)], pass_recv.at[part]
        ).wait()

    def z_filter(number, low, high):
        cells = jnp.concatenate([low, high], axis=1).reshape(2 * n_blk * HALF, 128).astype(BF16)
        z_pass[number * 128:(number + 1) * 128, :] = lax.dot_general(
            cells, z_mat[...], contract, preferred_element_type=F32
        )

    for four in range(2):
        z_filter(four, recv_first[:, four].astype(F32), recv_second[:, four].astype(F32))
    low = recv_second[:, 2].astype(F32)
    high = pltpu.roll(low.reshape(2 * n_blk * PART, 128), 96, 1).reshape(2 * n_blk, PART, 128)
    z_filter(2, low, high)

    turn = lax.rem(row, 4)

    def filtered(number):
        start = (number // 4) * 128 + lax.rem(turn + number % 4, 4) * 32
        return z_pass[pl.ds(pl.multiple_of(start, 32), 32), :]

    linear = [filtered(number) for number in range(3)]
    for number, (left, right) in enumerate(PRODUCT_PAIRS):
        direct_ref[number, 0] = filtered(3 + number)
        product_ref[number, 0] = linear[left] * linear[right]

    def sent(sem, count):
        pltpu.make_async_copy(gathered.at[pl.ds(0, count)], gathered.at[pl.ds(0, count)], sem).wait()

    sent(gather_send.at[4], 1)
    sent(gather_send.at[0], 25)
    for d, count in ((1, 40), (2, 36), (3, 32)):
        pl.when(there(pln + steps[d]))(functools.partial(sent, gather_send.at[d], count))
    for part, ref in ((0, send_first), (1, send_second)):
        pltpu.make_async_copy(
            ref.at[pl.ds(0, many)], ref.at[pl.ds(0, many)], pass_send.at[part]
        ).wait()


def solution(mesh):
    sizes = (mesh.shape["grp"], mesh.shape["row"], mesh.shape["col"])
    n_blk = sizes[0] * sizes[1]
    tile = (8, 128)

    def body(velocity, profile, x_filters, z_filter):
        vmem = pl.BlockSpec(memory_space=pltpu.VMEM)
        result = jax.ShapeDtypeStruct((6, 1, 32, 1024), F32)
        direct, product = pl.pallas_call(
            functools.partial(kernel, sizes),
            out_shape=(result, result),
            in_specs=[
                pl.BlockSpec(memory_space=pltpu.SMEM),
                vmem,
                pl.BlockSpec(memory_space=pl.ANY),
                pl.BlockSpec(memory_space=pl.ANY),
            ],
            out_specs=(vmem, vmem),
            scratch_shapes=[
                pltpu.VMEM((3, 256, 128), F32),
                pltpu.VMEM((2 * HALF + 1, 3) + tile, jnp.int16),
                pltpu.VMEM((CELLS + 1, 3) + tile, jnp.int16),
                pltpu.VMEM((CELLS, 3) + tile, F32),
                pltpu.VMEM((CELLS, 3) + tile, F32),
                pltpu.VMEM((CELLS, 3) + tile, F32),
                pltpu.VMEM((3, 256, 128), F32),
                pltpu.VMEM((9 * 2 * PART, 2048), BF16),
                pltpu.VMEM((2 * PART, 1024), F32),
                pltpu.VMEM((2, 1024, 1024), BF16),
                pltpu.VMEM((1024, 1024), BF16),
                pltpu.VMEM((2 * n_blk, 2) + tile, BF16),
                pltpu.VMEM((2 * n_blk, 3) + tile, BF16),
                pltpu.VMEM((2 * n_blk, 2) + tile, BF16),
                pltpu.VMEM((2 * n_blk, 3) + tile, BF16),
                pltpu.VMEM((384, 1024), F32),
                pltpu.SemaphoreType.DMA((2,)),
                pltpu.SemaphoreType.DMA((5,)),
                pltpu.SemaphoreType.DMA((2, ROWS)),
                pltpu.SemaphoreType.DMA,
                pltpu.SemaphoreType.DMA((2,)),
                pltpu.SemaphoreType.DMA((2,)),
                pltpu.SemaphoreType.DMA((2,)),
            ],
            compiler_params=pltpu.CompilerParams(
                collective_id=0, has_side_effects=True, vmem_limit_bytes=60000 * 1024
            ),
            name="subgrid",
        )(profile, velocity, x_filters, z_filter)
        return direct - product

    placed = (P(None, "col", ("grp", "row"), None), P("col"), P(), P())
    return jax.shard_map(
        body,
        mesh=mesh,
        in_specs=placed,
        out_specs=P(None, "col", ("grp", "row"), None),
        check_vma=False,
    )
```

```python
import functools

import jax
import jax.numpy as jnp
from jax import lax
from jax.experimental import pallas as pl
from jax.experimental.pallas import tpu as pltpu
from jax.sharding import PartitionSpec as P

F32 = jnp.float32
BF16 = jnp.bfloat16
MESH = pl.DeviceIdType.MESH
PRODUCT_PAIRS = ((0, 0), (0, 1), (0, 2), (1, 1), (1, 2), (2, 2))
FIELD_FACTORS = ((0,), (1,), (2,)) + PRODUCT_PAIRS

DEPTH = 3
HALF = 16
PART = 8
WIDE = HALF + 2 * DEPTH
ROWS = 2 + 2 * DEPTH
CELLS = ROWS * WIDE
CODE_MAX = 32767.0
BOUND = 8.0


def encode(value):
    root = jnp.sqrt(jnp.sqrt(jnp.abs(value) * (1.0 / BOUND)))
    code = (root * CODE_MAX + 0.5).astype(jnp.int32)
    return jnp.where(value < 0.0, -code, code).astype(jnp.int16)


def decode(code):
    root = code.astype(jnp.int32).astype(F32) * (1.0 / CODE_MAX)
    return (root * jnp.abs(root)) * (root * root * BOUND)


def kernel(
    sizes,
    profile_ref, velocity_ref, x_hbm, z_hbm, direct_ref, product_ref,
    spread, coded, gathered, wide, first, second, advanced, fields, last_low,
    x_mat, z_mat, send_first, send_second, recv_first, recv_second, z_pass,
    weight_sem, gather_send, gather_recv, profile_sem, local_sem, pass_send, pass_recv, word,
):
    n_grp, n_row, n_col = sizes
    n_blk, n_pln = n_grp * n_row, n_col // 2
    grp, row, col = lax.axis_index("grp"), lax.axis_index("row"), lax.axis_index("col")
    blk = grp * n_row + row
    pln, half = col // 2, col % 2
    other = 1 - half
    toward = 2 * half - 1

    def there(plane):
        return (plane >= 0) & (plane < n_pln)

    def device(block, plane, side):
        block = lax.rem(block + n_blk, n_blk)
        return (block // n_row, lax.rem(block, n_row), plane * 2 + side)

    barrier = pltpu.get_barrier_semaphore()

    def say(target):
        pl.semaphore_signal(barrier, inc=1, device_id=target, device_id_type=MESH)

    beside = blk + toward
    for step in (-1, 1):
        @pl.when(there(pln + step))
        def _(step=step):
            for side in (0, 1):
                say(device(blk, pln + step, side))
                say(device(beside, pln + step, side))

    @pl.when(there(pln - 2))
    def _():
        say(device(blk, pln - 2, 1))

    @pl.when(there(pln + 2))
    def _():
        say(device(blk, pln + 2, 0))

    around = [(grp, lax.rem(row + step, n_row), col) for step in (1, n_row - 1)]
    across = [
        (grp, row, pln * 2 + other),
        (grp + 1 - 2 * lax.rem(grp, 2), row, col),
        (lax.rem(grp + 2, n_grp), row, col),
    ]
    for target in around + across:
        say(target)
    for side in (0, 1):
        say(device(beside, pln, side))

    x_copy = pltpu.make_async_copy(x_hbm, x_mat, weight_sem.at[0])
    z_copy = pltpu.make_async_copy(z_hbm, z_mat, weight_sem.at[1])
    x_copy.start()
    z_copy.start()

    for group in range(4):
        for comp in range(3):
            for chunk in range(8):
                spread[comp, pl.ds(group * 64 + chunk, 8, stride=8), :] = velocity_ref[
                    comp, 0, group * 8:(group + 1) * 8, chunk * 128:(chunk + 1) * 128
                ]

    def encode_cells(step, carry):
        for cell in range(4):
            start = pl.multiple_of((step * 4 + cell) * 8, 8)
            for comp in range(3):
                coded[step * 4 + cell, comp] = encode(spread[comp, pl.ds(start, 8), :])
        return carry

    lax.fori_loop(0, 2 * HALF // 4, encode_cells, 0)
    own_profile = jnp.full((8, 128), profile_ref[0], jnp.int32)
    for comp in range(3):
        coded[2 * HALF, comp] = own_profile.astype(jnp.int16)

    partners = 7
    for step, count in ((toward, 4), (-toward, 4), (2 * toward, 2)):
        partners = partners + jnp.where(there(pln + step), count, 0)
    pl.semaphore_wait(barrier, partners)

    def give(source, count, cell, part, line, kind, target):
        pltpu.make_async_remote_copy(
            src_ref=coded.at[pl.ds(source, count)],
            dst_ref=gathered.at[pl.ds(line * WIDE + cell, count)],
            send_sem=gather_send.at[kind], recv_sem=gather_recv.at[part, line],
            device_id=target, device_id_type=MESH,
        ).start()

    pltpu.make_async_remote_copy(
        src_ref=coded.at[pl.ds(2 * HALF, 1)], dst_ref=gathered.at[pl.ds(CELLS, 1)],
        send_sem=gather_send.at[4], recv_sem=profile_sem,
        device_id=device(blk, pln, other), device_id_type=MESH,
    ).start()

    own_line = DEPTH + half
    lines = (own_line, 5 - 3 * half, 1 + 5 * half, 7 - 7 * half)
    steps = (0, toward, -toward, 2 * toward)
    for part in range(2):
        for d in range(4):
            def main(side, d=d, part=part):
                target = device(blk, pln + steps[d], side)
                if part == 0 and side == 0:
                    give(0, 11 - d, DEPTH, part, lines[d], d, target)
                elif part == 0:
                    give(13 + d, 14 - 2 * d, d, part, lines[d], d, target)
                elif side == 0:
                    give(11 - d, PART, 14 - d, part, lines[d], d, target)
                else:
                    give(27 - d, 5 + d, 14 - d, part, lines[d], d, target)

            def strip(d=d, part=part):
                if d == 3:
                    return
                if part == 0:
                    give(29 + d, 3 - d, d, part, lines[d], d, device(blk + 1, pln + steps[d], 0))
                else:
                    give(0, 3 - d, DEPTH + HALF, part, lines[d], d, device(blk - 1, pln + steps[d], 1))

            if d == 0:
                for side in (0, 1):
                    pl.when(half != side)(functools.partial(main, side))
                strip()
            else:
                @pl.when(there(pln + steps[d]))
                def _(main=main, strip=strip):
                    main(0)
                    main(1)
                    strip()

    present = [
        (2 * pln - DEPTH + line >= 0) & (2 * pln - DEPTH + line < n_col) for line in range(ROWS)
    ]
    inside = [jnp.where(known, 1.0, 0.0).astype(F32) for known in present]

    for line in (0, 1, 2, 5, 6, 7):
        @pl.when(jnp.logical_not(present[line]))
        def _(line=line):
            def clear(cell, carry):
                for comp in range(3):
                    wide[line * WIDE + cell, comp] = jnp.zeros((8, 128), F32)
                return carry

            lax.fori_loop(0, WIDE, clear, 0)

    def keep(cell, carry):
        start = pl.multiple_of(((HALF - DEPTH) * half + cell) * 8, 8)
        for comp in range(3):
            wide[own_line * WIDE + DEPTH * other + cell, comp] = spread[comp, pl.ds(start, 8), :]
        return carry

    lax.fori_loop(0, HALF + DEPTH, keep, 0)

    def tell(target, turn):
        pl.semaphore_signal(word.at[turn], inc=1, device_id=target, device_id_type=MESH)

    for turn in range(n_row // 2):
        for target in around:
            tell(target, turn)
        pl.semaphore_wait(word.at[turn], 2)
    for turn, target in enumerate(across):
        tell(target, n_row // 2 + turn)
        pl.semaphore_wait(word.at[n_row // 2 + turn], 1)

    def arrive(part, line, low, count):
        pltpu.make_async_copy(
            gathered.at[pl.ds(0, count)], gathered.at[pl.ds(0, count)], gather_recv.at[part, line]
        ).wait()
        per = 2 if count % 2 == 0 else 1

        def some(step, carry):
            for cell in range(per):
                here = line * WIDE + low + step * per + cell
                for comp in range(3):
                    wide[here, comp] = decode(gathered[here, comp])
            return carry

        lax.fori_loop(0, count // per, some, 0)

    lane = lax.broadcasted_iota(jnp.int32, (8, 128), 1)
    last_lane, first_lane = lane == 127, lane == 0

    def advance(source, scale, old, here):
        weight, advect = 0.2 * scale, 0.125 * scale
        center = [source[here, comp] for comp in range(3)]
        pairs = []
        for comp in range(3):
            scaled = center[comp] * advect
            pairs.append((weight - scaled, weight + scaled))
        results = []
        for comp in range(3):
            value = center[comp]
            ahead = pltpu.roll(value, 127, 1)
            ahead = jnp.where(last_lane, pltpu.roll(ahead, 7, 0), ahead)
            behind = pltpu.roll(value, 1, 1)
            behind = jnp.where(first_lane, pltpu.roll(behind, 1, 0), behind)
            total = (pairs[0][0] * ahead + pairs[0][1] * behind) + (
                pairs[1][0] * source[here + WIDE, comp] + pairs[1][1] * source[here - WIDE, comp]
            )
            total = total + (
                pairs[2][0] * source[here + 1, comp] + pairs[2][1] * source[here - 1, comp]
            )
            total = total - weight * value
            if old:
                total = total + old * wide[here, comp]
            results.append(total)
        return results

    def sweep(number, part, d):
        source = (wide, first, second)[number - 1]
        scale, old = ((1.0, None), (0.25, 0.75), (2.0 / 3.0, 1.0 / 3.0))[number - 1]
        low, high = ((d + number, 14 - d - number), (14 - d - number, 22 - d - number))[part]

        def two(step, carry):
            done = []
            for line in (DEPTH - d, DEPTH + 1 + d):
                for cell in range(2):
                    place = low + 2 * step + cell
                    done.append((line, place, advance(source, scale, old, line * WIDE + place)))
            for line, place, results in done:
                for comp in range(3):
                    value = results[comp]
                    if number == 3:
                        start = ((part * 2 + line - DEPTH) * PART + place - low) * 8
                        advanced[comp, pl.ds(pl.multiple_of(start, 8), 8), :] = value
                        continue
                    if d:
                        value = value * inside[line]
                    (first, second)[number - 1][line * WIDE + place, comp] = value
            return carry

        lax.fori_loop(0, (high - low) // 2, two, 0)

    wide_lane = lax.broadcasted_iota(jnp.int32, (2 * PART, 128), 1)
    quarter = wide_lane // 32
    small_quarter = lane // 32
    spot = 2 * blk + half

    def pass_part(part, one, zero):
        for chunk in range(8):
            comps = [
                advanced[comp, pl.ds(part * 128 + chunk, 2 * PART, stride=8), :] for comp in range(3)
            ]
            for number, factors in enumerate(FIELD_FACTORS):
                field = functools.reduce(lambda a, b: a * b, [comps[f] for f in factors])
                rows = slice(number * 2 * PART, (number + 1) * 2 * PART)
                fields[rows, chunk * 128:(chunk + 1) * 128] = (field * zero).astype(BF16)
                fields[rows, 1024 + chunk * 128:1024 + (chunk + 1) * 128] = (field * one).astype(BF16)
        send_ref = (send_first, send_second)[part]
        recv_ref = (recv_first, recv_second)[part]

        def outputs(step, carry):
            dest_grp = lax.rem(grp + 1 + step, n_grp)
            start = pl.multiple_of(dest_grp * n_row * 32, 256)
            contract = (((1,), (1,)), ((), ()))
            passed = lax.dot_general(
                fields[:, 0:1024], x_mat[0, pl.ds(start, 256), :], contract,
                preferred_element_type=F32,
            ) + lax.dot_general(
                fields[:, 1024:2048], x_mat[1, pl.ds(start, 256), :], contract,
                preferred_element_type=F32,
            )
            if part == 0:
                last_low[:, pl.ds(start, 256)] = passed[128:144]
            else:
                lows = last_low[:, pl.ds(start, 256)]
            for tile in range(2):
                lanes = slice(tile * 128, (tile + 1) * 128)
                for four in range(2):
                    turned = []
                    for k in range(4):
                        piece = passed[(four * 4 + k) * 16:(four * 4 + k + 1) * 16, lanes]
                        turned.append(pltpu.roll(piece, 32 * k, 1) if k else piece)
                    for place in range(4):
                        mixed = turned[3]
                        for k in range(3):
                            mixed = jnp.where(quarter == (place + k) % 4, turned[k], mixed)
                        dest = dest_grp * n_row + tile * 4 + place
                        send_ref[dest, four] = mixed[0:PART].astype(BF16)
                        send_ref[n_blk + dest, four] = mixed[PART:2 * PART].astype(BF16)
                if part == 1:
                    for line in range(2):
                        rows = slice(line * PART, (line + 1) * PART)
                        high = pltpu.roll(passed[128:144, lanes][rows], 32, 1)
                        low = lows[rows, lanes]
                        for place in range(4):
                            dest = dest_grp * n_row + tile * 4 + place
                            send_ref[line * n_blk + dest, 2] = jnp.where(
                                small_quarter == place, low, high
                            ).astype(BF16)
            for off in (4, 3, 5, 2, 6, 1, 7, 0):
                dest_row = lax.rem(row + off, n_row)
                dest = dest_grp * n_row + dest_row
                for line in range(2):
                    target = (dest_grp, dest_row, 2 * pln + line)

                    def send(line=line, target=target, dest=dest):
                        pltpu.make_async_remote_copy(
                            src_ref=send_ref.at[line * n_blk + dest], dst_ref=recv_ref.at[spot],
                            send_sem=pass_send.at[part], recv_sem=pass_recv.at[part],
                            device_id=target, device_id_type=MESH,
                        ).start()

                    if off:
                        send()
                    else:
                        pl.when((dest != blk) | (half != line))(send)
            return carry

        lax.fori_loop(0, n_grp, outputs, 0)
        stay = pltpu.make_async_copy(
            send_ref.at[half * n_blk + blk], recv_ref.at[spot], local_sem.at[part]
        )
        stay.start()
        return stay

    stays = []
    for part in range(2):
        for d in range(4):
            if d == 0:
                arrive(part, 4 - half, (0, 14)[part], (14, PART)[part])
                pl.when(half == part)(
                    functools.partial(arrive, part, own_line, (0, DEPTH + HALF)[part], DEPTH)
                )
                continue
            for line in (DEPTH - d, DEPTH + 1 + d):
                pl.when(present[line])(
                    functools.partial(arrive, part, line, (d, 14 - d)[part], (14 - 2 * d, PART)[part])
                )
            for number in range(1, d + 1):
                sweep(number, part, d - number)
        if part == 0:
            pltpu.make_async_copy(
                gathered.at[pl.ds(0, 1)], gathered.at[pl.ds(0, 1)], profile_sem
            ).wait()
            pair_profile = gathered[CELLS, 0].astype(jnp.int32)
            even = jnp.where(half == 0, own_profile, pair_profile).astype(F32)
            odd = jnp.where(half == 0, pair_profile, own_profile).astype(F32)
            one = jnp.concatenate([even, odd], axis=0)
            x_copy.wait()
        stays.append(pass_part(part, one, 1.0 - one))
    z_copy.wait()

    contract = (((0,), (1,)), ((), ()))
    many = 2 * n_blk - 1
    for part, ref in ((0, recv_first), (1, recv_second)):
        stays[part].wait()
        pltpu.make_async_copy(
            ref.at[pl.ds(0, many)], ref.at[pl.ds(0, many)], pass_recv.at[part]
        ).wait()

    def z_filter(number, low, high):
        cells = jnp.concatenate([low, high], axis=1).reshape(2 * n_blk * HALF, 128).astype(BF16)
        z_pass[number * 128:(number + 1) * 128, :] = lax.dot_general(
            cells, z_mat[...], contract, preferred_element_type=F32
        )

    for four in range(2):
        z_filter(four, recv_first[:, four].astype(F32), recv_second[:, four].astype(F32))
    low = recv_second[:, 2].astype(F32)
    high = pltpu.roll(low.reshape(2 * n_blk * PART, 128), 96, 1).reshape(2 * n_blk, PART, 128)
    z_filter(2, low, high)

    turn = lax.rem(row, 4)

    def filtered(number):
        start = (number // 4) * 128 + lax.rem(turn + number % 4, 4) * 32
        return z_pass[pl.ds(pl.multiple_of(start, 32), 32), :]

    linear = [filtered(number) for number in range(3)]
    for number, (left, right) in enumerate(PRODUCT_PAIRS):
        direct_ref[number, 0] = filtered(3 + number)
        product_ref[number, 0] = linear[left] * linear[right]

    def sent(sem, count):
        pltpu.make_async_copy(gathered.at[pl.ds(0, count)], gathered.at[pl.ds(0, count)], sem).wait()

    sent(gather_send.at[4], 1)
    sent(gather_send.at[0], 25)
    for d, count in ((1, 40), (2, 36), (3, 32)):
        pl.when(there(pln + steps[d]))(functools.partial(sent, gather_send.at[d], count))
    for part, ref in ((0, send_first), (1, send_second)):
        pltpu.make_async_copy(
            ref.at[pl.ds(0, many)], ref.at[pl.ds(0, many)], pass_send.at[part]
        ).wait()


def solution(mesh):
    sizes = (mesh.shape["grp"], mesh.shape["row"], mesh.shape["col"])
    n_blk = sizes[0] * sizes[1]
    tile = (8, 128)

    def body(velocity, profile, x_filters, z_filter):
        vmem = pl.BlockSpec(memory_space=pltpu.VMEM)
        result = pltpu.VMEM((6, 1, 32, 1024), F32)
        direct, product = pl.pallas_call(
            functools.partial(kernel, sizes),
            out_shape=(result, result),
            in_specs=[
                pl.BlockSpec(memory_space=pltpu.SMEM),
                vmem,
                pl.BlockSpec(memory_space=pl.ANY),
                pl.BlockSpec(memory_space=pl.ANY),
            ],
            out_specs=(vmem, vmem),
            scratch_shapes=[
                pltpu.VMEM((3, 256, 128), F32),
                pltpu.VMEM((2 * HALF + 1, 3) + tile, jnp.int16),
                pltpu.VMEM((CELLS + 1, 3) + tile, jnp.int16),
                pltpu.VMEM((CELLS, 3) + tile, F32),
                pltpu.VMEM((CELLS, 3) + tile, F32),
                pltpu.VMEM((CELLS, 3) + tile, F32),
                pltpu.VMEM((3, 256, 128), F32),
                pltpu.VMEM((9 * 2 * PART, 2048), BF16),
                pltpu.VMEM((2 * PART, 1024), F32),
                pltpu.VMEM((2, 1024, 1024), BF16),
                pltpu.VMEM((1024, 1024), BF16),
                pltpu.VMEM((2 * n_blk, 2) + tile, BF16),
                pltpu.VMEM((2 * n_blk, 3) + tile, BF16),
                pltpu.VMEM((2 * n_blk, 2) + tile, BF16),
                pltpu.VMEM((2 * n_blk, 3) + tile, BF16),
                pltpu.VMEM((384, 1024), F32),
                pltpu.SemaphoreType.DMA((2,)),
                pltpu.SemaphoreType.DMA((5,)),
                pltpu.SemaphoreType.DMA((2, ROWS)),
                pltpu.SemaphoreType.DMA,
                pltpu.SemaphoreType.DMA((2,)),
                pltpu.SemaphoreType.DMA((2,)),
                pltpu.SemaphoreType.DMA((2,)),
                pltpu.SemaphoreType.REGULAR((sizes[1] // 2 + 3,)),
            ],
            compiler_params=pltpu.CompilerParams(
                collective_id=0, has_side_effects=True, vmem_limit_bytes=60000 * 1024
            ),
            name="subgrid",
        )(profile, velocity, x_filters, z_filter)
        return direct - product

    placed = (P(None, "col", ("grp", "row"), None), P("col"), P(), P())
    return jax.shard_map(
        body,
        mesh=mesh,
        in_specs=placed,
        out_specs=P(None, "col", ("grp", "row"), None),
        check_vma=False,
    )
```

```python
import functools

import jax
import jax.numpy as jnp
from jax import lax
from jax.experimental import pallas as pl
from jax.experimental.pallas import tpu as pltpu
from jax.sharding import PartitionSpec as P

F32 = jnp.float32
BF16 = jnp.bfloat16
MESH = pl.DeviceIdType.MESH
PRODUCT_PAIRS = ((0, 0), (0, 1), (0, 2), (1, 1), (1, 2), (2, 2))
FIELD_FACTORS = ((0,), (1,), (2,)) + PRODUCT_PAIRS

DEPTH = 3
HALF = 16
PART = 8
WIDE = HALF + 2 * DEPTH
ROWS = 2 + 2 * DEPTH
CELLS = ROWS * WIDE
CODE_MAX = 32767.0
BOUND = 8.0


def encode(value):
    root = jnp.sqrt(jnp.sqrt(jnp.abs(value) * (1.0 / BOUND)))
    code = (root * CODE_MAX + 0.5).astype(jnp.int32)
    return jnp.where(value < 0.0, -code, code).astype(jnp.int16)


def decode(code):
    root = code.astype(jnp.int32).astype(F32) * (1.0 / CODE_MAX)
    return (root * jnp.abs(root)) * (root * root * BOUND)


def kernel(
    sizes,
    profile_hbm, velocity_ref, x_hbm, z_hbm, direct_ref, product_ref,
    spread, coded, gathered, wide, first, second, advanced, fields, last_low,
    x_mat, z_mat, send_first, send_second, recv_first, recv_second, z_pass,
    weight_sem, gather_send, gather_recv, profile_sem, local_sem, pass_send, pass_recv, word, profile_word,
):
    n_grp, n_row, n_col = sizes
    n_blk, n_pln = n_grp * n_row, n_col // 2
    grp, row, col = lax.axis_index("grp"), lax.axis_index("row"), lax.axis_index("col")
    blk = grp * n_row + row
    pln, half = col // 2, col % 2
    other = 1 - half
    toward = 2 * half - 1

    def there(plane):
        return (plane >= 0) & (plane < n_pln)

    def device(block, plane, side):
        block = lax.rem(block + n_blk, n_blk)
        return (block // n_row, lax.rem(block, n_row), plane * 2 + side)

    barrier = pltpu.get_barrier_semaphore()

    def say(target):
        pl.semaphore_signal(barrier, inc=1, device_id=target, device_id_type=MESH)

    beside = blk + toward
    for step in (-1, 1):
        @pl.when(there(pln + step))
        def _(step=step):
            for side in (0, 1):
                say(device(blk, pln + step, side))
                say(device(beside, pln + step, side))

    @pl.when(there(pln - 2))
    def _():
        say(device(blk, pln - 2, 1))

    @pl.when(there(pln + 2))
    def _():
        say(device(blk, pln + 2, 0))

    around = [(grp, lax.rem(row + step, n_row), col) for step in (1, n_row - 1)]
    across = [(grp, row, pln * 2 + other)] + [
        (lax.rem(grp + step, n_grp), row, pln * 2 + side) for step in range(1, n_grp) for side in (0, 1)
    ]
    for target in around + across:
        say(target)
    for side in (0, 1):
        say(device(beside, pln, side))

    x_copy = pltpu.make_async_copy(x_hbm, x_mat, weight_sem.at[0])
    z_copy = pltpu.make_async_copy(z_hbm, z_mat, weight_sem.at[1])
    profile_copy = pltpu.make_async_copy(profile_hbm, profile_word, weight_sem.at[2])
    profile_copy.start()
    x_copy.start()
    z_copy.start()

    for group in range(4):
        for comp in range(3):
            for chunk in range(8):
                spread[comp, pl.ds(group * 64 + chunk, 8, stride=8), :] = velocity_ref[
                    comp, 0, group * 8:(group + 1) * 8, chunk * 128:(chunk + 1) * 128
                ]

    def encode_cells(step, carry):
        for cell in range(4):
            start = pl.multiple_of((step * 4 + cell) * 8, 8)
            for comp in range(3):
                coded[step * 4 + cell, comp] = encode(spread[comp, pl.ds(start, 8), :])
        return carry

    lax.fori_loop(0, 2 * HALF // 4, encode_cells, 0)
    profile_copy.wait()
    own_profile = jnp.full((8, 128), profile_word[0], jnp.int32)
    for comp in range(3):
        coded[2 * HALF, comp] = own_profile.astype(jnp.int16)

    partners = len(across) + len(around) + 2
    for step, count in ((toward, 4), (-toward, 4), (2 * toward, 2)):
        partners = partners + jnp.where(there(pln + step), count, 0)
    pl.semaphore_wait(barrier, partners)

    def give(source, count, cell, part, line, kind, target):
        pltpu.make_async_remote_copy(
            src_ref=coded.at[pl.ds(source, count)],
            dst_ref=gathered.at[pl.ds(line * WIDE + cell, count)],
            send_sem=gather_send.at[kind], recv_sem=gather_recv.at[part, line],
            device_id=target, device_id_type=MESH,
        ).start()

    pltpu.make_async_remote_copy(
        src_ref=coded.at[pl.ds(2 * HALF, 1)], dst_ref=gathered.at[pl.ds(CELLS, 1)],
        send_sem=gather_send.at[4], recv_sem=profile_sem,
        device_id=device(blk, pln, other), device_id_type=MESH,
    ).start()

    own_line = DEPTH + half
    lines = (own_line, 5 - 3 * half, 1 + 5 * half, 7 - 7 * half)
    steps = (0, toward, -toward, 2 * toward)
    for part in range(2):
        for d in range(4):
            def main(side, d=d, part=part):
                target = device(blk, pln + steps[d], side)
                if part == 0 and side == 0:
                    give(0, 11 - d, DEPTH, part, lines[d], d, target)
                elif part == 0:
                    give(13 + d, 14 - 2 * d, d, part, lines[d], d, target)
                elif side == 0:
                    give(11 - d, PART, 14 - d, part, lines[d], d, target)
                else:
                    give(27 - d, 5 + d, 14 - d, part, lines[d], d, target)

            def strip(d=d, part=part):
                if d == 3:
                    return
                if part == 0:
                    give(29 + d, 3 - d, d, part, lines[d], d, device(blk + 1, pln + steps[d], 0))
                else:
                    give(0, 3 - d, DEPTH + HALF, part, lines[d], d, device(blk - 1, pln + steps[d], 1))

            if d == 0:
                for side in (0, 1):
                    pl.when(half != side)(functools.partial(main, side))
                strip()
            else:
                @pl.when(there(pln + steps[d]))
                def _(main=main, strip=strip):
                    main(0)
                    main(1)
                    strip()

    present = [
        (2 * pln - DEPTH + line >= 0) & (2 * pln - DEPTH + line < n_col) for line in range(ROWS)
    ]
    inside = [jnp.where(known, 1.0, 0.0).astype(F32) for known in present]

    for line in (0, 1, 2, 5, 6, 7):
        @pl.when(jnp.logical_not(present[line]))
        def _(line=line):
            def clear(cell, carry):
                for comp in range(3):
                    wide[line * WIDE + cell, comp] = jnp.zeros((8, 128), F32)
                return carry

            lax.fori_loop(0, WIDE, clear, 0)

    def keep(cell, carry):
        start = pl.multiple_of(((HALF - DEPTH) * half + cell) * 8, 8)
        for comp in range(3):
            wide[own_line * WIDE + DEPTH * other + cell, comp] = spread[comp, pl.ds(start, 8), :]
        return carry

    lax.fori_loop(0, HALF + DEPTH, keep, 0)

    def tell(target, turn):
        pl.semaphore_signal(word.at[turn], inc=1, device_id=target, device_id_type=MESH)

    def tell_all(turn):
        for target in around if turn else across:
            tell(target, turn)

    def hear_all(turn):
        pl.semaphore_wait(word.at[turn], len(around if turn else across))

    turns = n_row // 2 + 1
    tell_all(0)

    def arrive(part, line, low, count):
        pltpu.make_async_copy(
            gathered.at[pl.ds(0, count)], gathered.at[pl.ds(0, count)], gather_recv.at[part, line]
        ).wait()
        per = 2 if count % 2 == 0 else 1

        def some(step, carry):
            for cell in range(per):
                here = line * WIDE + low + step * per + cell
                for comp in range(3):
                    wide[here, comp] = decode(gathered[here, comp])
            return carry

        lax.fori_loop(0, count // per, some, 0)

    lane = lax.broadcasted_iota(jnp.int32, (8, 128), 1)
    last_lane, first_lane = lane == 127, lane == 0

    def advance(source, scale, old, here):
        weight, advect = 0.2 * scale, 0.125 * scale
        center = [source[here, comp] for comp in range(3)]
        pairs = []
        for comp in range(3):
            scaled = center[comp] * advect
            pairs.append((weight - scaled, weight + scaled))
        results = []
        for comp in range(3):
            value = center[comp]
            ahead = pltpu.roll(value, 127, 1)
            ahead = jnp.where(last_lane, pltpu.roll(ahead, 7, 0), ahead)
            behind = pltpu.roll(value, 1, 1)
            behind = jnp.where(first_lane, pltpu.roll(behind, 1, 0), behind)
            total = (pairs[0][0] * ahead + pairs[0][1] * behind) + (
                pairs[1][0] * source[here + WIDE, comp] + pairs[1][1] * source[here - WIDE, comp]
            )
            total = total + (
                pairs[2][0] * source[here + 1, comp] + pairs[2][1] * source[here - 1, comp]
            )
            total = total - weight * value
            if old:
                total = total + old * wide[here, comp]
            results.append(total)
        return results

    def sweep(number, part, d):
        source = (wide, first, second)[number - 1]
        scale, old = ((1.0, None), (0.25, 0.75), (2.0 / 3.0, 1.0 / 3.0))[number - 1]
        low, high = ((d + number, 14 - d - number), (14 - d - number, 22 - d - number))[part]

        def two(step, carry):
            done = []
            for line in (DEPTH - d, DEPTH + 1 + d):
                for cell in range(2):
                    place = low + 2 * step + cell
                    done.append((line, place, advance(source, scale, old, line * WIDE + place)))
            for line, place, results in done:
                for comp in range(3):
                    value = results[comp]
                    if number == 3:
                        start = ((part * 2 + line - DEPTH) * PART + place - low) * 8
                        advanced[comp, pl.ds(pl.multiple_of(start, 8), 8), :] = value
                        continue
                    if d:
                        value = value * inside[line]
                    (first, second)[number - 1][line * WIDE + place, comp] = value
            return carry

        lax.fori_loop(0, (high - low) // 2, two, 0)

    wide_lane = lax.broadcasted_iota(jnp.int32, (2 * PART, 128), 1)
    quarter = wide_lane // 32
    small_quarter = lane // 32
    spot = 2 * blk + half

    def pass_part(part, one, zero):
        for chunk in range(8):
            comps = [
                advanced[comp, pl.ds(part * 128 + chunk, 2 * PART, stride=8), :] for comp in range(3)
            ]
            for number, factors in enumerate(FIELD_FACTORS):
                field = functools.reduce(lambda a, b: a * b, [comps[f] for f in factors])
                rows = slice(number * 2 * PART, (number + 1) * 2 * PART)
                fields[rows, chunk * 128:(chunk + 1) * 128] = (field * zero).astype(BF16)
                fields[rows, 1024 + chunk * 128:1024 + (chunk + 1) * 128] = (field * one).astype(BF16)
        send_ref = (send_first, send_second)[part]
        recv_ref = (recv_first, recv_second)[part]

        def outputs(step, carry):
            dest_grp = lax.rem(grp + 1 + step, n_grp)
            start = pl.multiple_of(dest_grp * n_row * 32, 256)
            contract = (((1,), (1,)), ((), ()))
            passed = lax.dot_general(
                fields[:, 0:1024], x_mat[0, pl.ds(start, 256), :], contract,
                preferred_element_type=F32,
            ) + lax.dot_general(
                fields[:, 1024:2048], x_mat[1, pl.ds(start, 256), :], contract,
                preferred_element_type=F32,
            )
            if part == 0:
                last_low[:, pl.ds(start, 256)] = passed[128:144]
            else:
                lows = last_low[:, pl.ds(start, 256)]
            for tile in range(2):
                lanes = slice(tile * 128, (tile + 1) * 128)
                for four in range(2):
                    turned = []
                    for k in range(4):
                        piece = passed[(four * 4 + k) * 16:(four * 4 + k + 1) * 16, lanes]
                        turned.append(pltpu.roll(piece, 32 * k, 1) if k else piece)
                    for place in range(4):
                        mixed = turned[3]
                        for k in range(3):
                            mixed = jnp.where(quarter == (place + k) % 4, turned[k], mixed)
                        dest = dest_grp * n_row + tile * 4 + place
                        send_ref[dest, four] = mixed[0:PART].astype(BF16)
                        send_ref[n_blk + dest, four] = mixed[PART:2 * PART].astype(BF16)
                if part == 1:
                    for line in range(2):
                        rows = slice(line * PART, (line + 1) * PART)
                        high = pltpu.roll(passed[128:144, lanes][rows], 32, 1)
                        low = lows[rows, lanes]
                        for place in range(4):
                            dest = dest_grp * n_row + tile * 4 + place
                            send_ref[line * n_blk + dest, 2] = jnp.where(
                                small_quarter == place, low, high
                            ).astype(BF16)
            for off in (4, 3, 5, 2, 6, 1, 7, 0):
                dest_row = lax.rem(row + off, n_row)
                dest = dest_grp * n_row + dest_row
                for line in range(2):
                    target = (dest_grp, dest_row, 2 * pln + line)

                    def send(line=line, target=target, dest=dest):
                        pltpu.make_async_remote_copy(
                            src_ref=send_ref.at[line * n_blk + dest], dst_ref=recv_ref.at[spot],
                            send_sem=pass_send.at[part], recv_sem=pass_recv.at[part],
                            device_id=target, device_id_type=MESH,
                        ).start()

                    if off:
                        send()
                    else:
                        pl.when((dest != blk) | (half != line))(send)
            return carry

        lax.fori_loop(0, n_grp, outputs, 0)
        stay = pltpu.make_async_copy(
            send_ref.at[half * n_blk + blk], recv_ref.at[spot], local_sem.at[part]
        )
        stay.start()
        return stay

    stays = []
    for part in range(2):
        for d in range(4):
            if d == 0:
                arrive(part, 4 - half, (0, 14)[part], (14, PART)[part])
                pl.when(half == part)(
                    functools.partial(arrive, part, own_line, (0, DEPTH + HALF)[part], DEPTH)
                )
                if part == 0:
                    hear_all(0)
                    tell_all(1)
                continue
            for line in (DEPTH - d, DEPTH + 1 + d):
                pl.when(present[line])(
                    functools.partial(arrive, part, line, (d, 14 - d)[part], (14 - 2 * d, PART)[part])
                )
            if part == 0:
                hear_all(d)
                tell_all(d + 1)
            for number in range(1, d + 1):
                sweep(number, part, d - number)
        if part == 0:
            pltpu.make_async_copy(
                gathered.at[pl.ds(0, 1)], gathered.at[pl.ds(0, 1)], profile_sem
            ).wait()
            pair_profile = gathered[CELLS, 0].astype(jnp.int32)
            even = jnp.where(half == 0, own_profile, pair_profile).astype(F32)
            odd = jnp.where(half == 0, pair_profile, own_profile).astype(F32)
            one = jnp.concatenate([even, odd], axis=0)
            x_copy.wait()
            for turn in range(4, turns - 1):
                hear_all(turn)
                tell_all(turn + 1)
            hear_all(turns - 1)
        stays.append(pass_part(part, one, 1.0 - one))
    z_copy.wait()

    contract = (((0,), (1,)), ((), ()))
    many = 2 * n_blk - 1
    for part, ref in ((0, recv_first), (1, recv_second)):
        stays[part].wait()
        pltpu.make_async_copy(
            ref.at[pl.ds(0, many)], ref.at[pl.ds(0, many)], pass_recv.at[part]
        ).wait()

    def z_filter(number, low, high):
        cells = jnp.concatenate([low, high], axis=1).reshape(2 * n_blk * HALF, 128).astype(BF16)
        z_pass[number * 128:(number + 1) * 128, :] = lax.dot_general(
            cells, z_mat[...], contract, preferred_element_type=F32
        )

    for four in range(2):
        z_filter(four, recv_first[:, four].astype(F32), recv_second[:, four].astype(F32))
    low = recv_second[:, 2].astype(F32)
    high = pltpu.roll(low.reshape(2 * n_blk * PART, 128), 96, 1).reshape(2 * n_blk, PART, 128)
    z_filter(2, low, high)

    turn = lax.rem(row, 4)

    def filtered(number):
        start = (number // 4) * 128 + lax.rem(turn + number % 4, 4) * 32
        return z_pass[pl.ds(pl.multiple_of(start, 32), 32), :]

    linear = [filtered(number) for number in range(3)]
    for number, (left, right) in enumerate(PRODUCT_PAIRS):
        direct_ref[number, 0] = filtered(3 + number)
        product_ref[number, 0] = linear[left] * linear[right]

    def sent(sem, count):
        pltpu.make_async_copy(gathered.at[pl.ds(0, count)], gathered.at[pl.ds(0, count)], sem).wait()

    sent(gather_send.at[4], 1)
    sent(gather_send.at[0], 25)
    for d, count in ((1, 40), (2, 36), (3, 32)):
        pl.when(there(pln + steps[d]))(functools.partial(sent, gather_send.at[d], count))
    for part, ref in ((0, send_first), (1, send_second)):
        pltpu.make_async_copy(
            ref.at[pl.ds(0, many)], ref.at[pl.ds(0, many)], pass_send.at[part]
        ).wait()


def solution(mesh):
    sizes = (mesh.shape["grp"], mesh.shape["row"], mesh.shape["col"])
    n_blk = sizes[0] * sizes[1]
    tile = (8, 128)

    def body(velocity, profile, x_filters, z_filter):
        vmem = pl.BlockSpec(memory_space=pltpu.VMEM)
        result = pltpu.VMEM((6, 1, 32, 1024), F32)
        direct, product = pl.pallas_call(
            functools.partial(kernel, sizes),
            out_shape=(result, result),
            in_specs=[
                pl.BlockSpec(memory_space=pl.ANY),
                vmem,
                pl.BlockSpec(memory_space=pl.ANY),
                pl.BlockSpec(memory_space=pl.ANY),
            ],
            out_specs=(vmem, vmem),
            scratch_shapes=[
                pltpu.VMEM((3, 256, 128), F32),
                pltpu.VMEM((2 * HALF + 1, 3) + tile, jnp.int16),
                pltpu.VMEM((CELLS + 1, 3) + tile, jnp.int16),
                pltpu.VMEM((CELLS, 3) + tile, F32),
                pltpu.VMEM((CELLS, 3) + tile, F32),
                pltpu.VMEM((CELLS, 3) + tile, F32),
                pltpu.VMEM((3, 256, 128), F32),
                pltpu.VMEM((9 * 2 * PART, 2048), BF16),
                pltpu.VMEM((2 * PART, 1024), F32),
                pltpu.VMEM((2, 1024, 1024), BF16),
                pltpu.VMEM((1024, 1024), BF16),
                pltpu.VMEM((2 * n_blk, 2) + tile, BF16),
                pltpu.VMEM((2 * n_blk, 3) + tile, BF16),
                pltpu.VMEM((2 * n_blk, 2) + tile, BF16),
                pltpu.VMEM((2 * n_blk, 3) + tile, BF16),
                pltpu.VMEM((384, 1024), F32),
                pltpu.SemaphoreType.DMA((3,)),
                pltpu.SemaphoreType.DMA((5,)),
                pltpu.SemaphoreType.DMA((2, ROWS)),
                pltpu.SemaphoreType.DMA,
                pltpu.SemaphoreType.DMA((2,)),
                pltpu.SemaphoreType.DMA((2,)),
                pltpu.SemaphoreType.DMA((2,)),
                pltpu.SemaphoreType.REGULAR((sizes[1] // 2 + 1,)),
                pltpu.SMEM((1,), jnp.int32),
            ],
            compiler_params=pltpu.CompilerParams(
                collective_id=0, has_side_effects=True, vmem_limit_bytes=60000 * 1024
            ),
            name="subgrid",
        )(profile, velocity, x_filters, z_filter)
        return direct - product

    placed = (P(None, "col", ("grp", "row"), None), P("col"), P(), P())
    return jax.shard_map(
        body,
        mesh=mesh,
        in_specs=placed,
        out_specs=P(None, "col", ("grp", "row"), None),
        check_vma=False,
    )
```

```python
import functools

import jax
import jax.numpy as jnp
from jax import lax
from jax.experimental import pallas as pl
from jax.experimental.pallas import tpu as pltpu
from jax.sharding import PartitionSpec as P

F32 = jnp.float32
BF16 = jnp.bfloat16
MESH = pl.DeviceIdType.MESH
PRODUCT_PAIRS = ((0, 0), (0, 1), (0, 2), (1, 1), (1, 2), (2, 2))
FIELD_FACTORS = ((0,), (1,), (2,)) + PRODUCT_PAIRS

DEPTH = 3
HALF = 16
PART = 8
WIDE = HALF + 2 * DEPTH
ROWS = 2 + 2 * DEPTH
CELLS = ROWS * WIDE
CODE_MAX = 32767.0
BOUND = 8.0


def encode(value):
    root = jnp.sqrt(jnp.sqrt(jnp.abs(value) * (1.0 / BOUND)))
    code = (root * CODE_MAX + 0.5).astype(jnp.int32)
    return jnp.where(value < 0.0, -code, code).astype(jnp.int16)


def decode(code):
    root = code.astype(jnp.int32).astype(F32) * (1.0 / CODE_MAX)
    return (root * jnp.abs(root)) * (root * root * BOUND)


def kernel(
    sizes,
    profile_ref, velocity_ref, x_hbm, z_hbm, direct_ref, product_ref,
    spread, coded, gathered, wide, first, second, advanced, fields, last_low,
    x_mat, z_mat, send_first, send_second, recv_first, recv_second, z_pass, order, z_turned,
    weight_sem, gather_send, gather_recv, profile_sem, local_sem, pass_send, pass_recv,
):
    n_grp, n_row, n_col = sizes
    n_blk, n_pln = n_grp * n_row, n_col // 2
    grp, row, col = lax.axis_index("grp"), lax.axis_index("row"), lax.axis_index("col")
    blk = grp * n_row + row
    pln, half = col // 2, col % 2
    other = 1 - half
    toward = 2 * half - 1

    def there(plane):
        return (plane >= 0) & (plane < n_pln)

    def device(block, plane, side):
        block = lax.rem(block + n_blk, n_blk)
        return (block // n_row, lax.rem(block, n_row), plane * 2 + side)

    barrier = pltpu.get_barrier_semaphore()

    def say(target):
        pl.semaphore_signal(barrier, inc=1, device_id=target, device_id_type=MESH)

    beside = blk + toward
    for step in (-1, 1):
        @pl.when(there(pln + step))
        def _(step=step):
            for side in (0, 1):
                say(device(blk, pln + step, side))
                say(device(beside, pln + step, side))

    @pl.when(there(pln - 2))
    def _():
        say(device(blk, pln - 2, 1))

    @pl.when(there(pln + 2))
    def _():
        say(device(blk, pln + 2, 0))

    say(device(blk, pln, other))

    def say_block(step, carry):
        say(device(blk + step, pln, 0))
        say(device(blk + step, pln, 1))
        return carry

    lax.fori_loop(1, n_blk, say_block, 0)

    x_copy = pltpu.make_async_copy(x_hbm, x_mat, weight_sem.at[0])
    z_copy = pltpu.make_async_copy(z_hbm, z_mat, weight_sem.at[1])
    x_copy.start()
    z_copy.start()

    for group in range(4):
        for comp in range(3):
            for chunk in range(8):
                spread[comp, pl.ds(group * 64 + chunk, 8, stride=8), :] = velocity_ref[
                    comp, 0, group * 8:(group + 1) * 8, chunk * 128:(chunk + 1) * 128
                ]

    def encode_cells(step, carry):
        for cell in range(4):
            start = pl.multiple_of((step * 4 + cell) * 8, 8)
            for comp in range(3):
                coded[step * 4 + cell, comp] = encode(spread[comp, pl.ds(start, 8), :])
        return carry

    lax.fori_loop(0, 2 * HALF // 4, encode_cells, 0)
    own_profile = jnp.full((8, 128), profile_ref[0], jnp.int32)
    for comp in range(3):
        coded[2 * HALF, comp] = own_profile.astype(jnp.int16)

    partners = 2 * n_blk - 1
    for step, count in ((toward, 4), (-toward, 4), (2 * toward, 2)):
        partners = partners + jnp.where(there(pln + step), count, 0)
    pl.semaphore_wait(barrier, partners)

    def give(source, count, cell, part, line, kind, target):
        pltpu.make_async_remote_copy(
            src_ref=coded.at[pl.ds(source, count)],
            dst_ref=gathered.at[pl.ds(line * WIDE + cell, count)],
            send_sem=gather_send.at[kind], recv_sem=gather_recv.at[part, line],
            device_id=target, device_id_type=MESH,
        ).start()

    pltpu.make_async_remote_copy(
        src_ref=coded.at[pl.ds(2 * HALF, 1)], dst_ref=gathered.at[pl.ds(CELLS, 1)],
        send_sem=gather_send.at[4], recv_sem=profile_sem,
        device_id=device(blk, pln, other), device_id_type=MESH,
    ).start()

    own_line = DEPTH + half
    lines = (own_line, 5 - 3 * half, 1 + 5 * half, 7 - 7 * half)
    steps = (0, toward, -toward, 2 * toward)
    for part in range(2):
        for d in range(4):
            def main(side, d=d, part=part):
                target = device(blk, pln + steps[d], side)
                if part == 0 and side == 0:
                    give(0, 11 - d, DEPTH, part, lines[d], d, target)
                elif part == 0:
                    give(13 + d, 14 - 2 * d, d, part, lines[d], d, target)
                elif side == 0:
                    give(11 - d, PART, 14 - d, part, lines[d], d, target)
                else:
                    give(27 - d, 5 + d, 14 - d, part, lines[d], d, target)

            def strip(d=d, part=part):
                if d == 3:
                    return
                if part == 0:
                    give(29 + d, 3 - d, d, part, lines[d], d, device(blk + 1, pln + steps[d], 0))
                else:
                    give(0, 3 - d, DEPTH + HALF, part, lines[d], d, device(blk - 1, pln + steps[d], 1))

            if d == 0:
                for side in (0, 1):
                    pl.when(half != side)(functools.partial(main, side))
                strip()
            else:
                @pl.when(there(pln + steps[d]))
                def _(main=main, strip=strip):
                    main(0)
                    main(1)
                    strip()

    present = [
        (2 * pln - DEPTH + line >= 0) & (2 * pln - DEPTH + line < n_col) for line in range(ROWS)
    ]
    inside = [jnp.where(known, 1.0, 0.0).astype(F32) for known in present]

    for line in (0, 1, 2, 5, 6, 7):
        @pl.when(jnp.logical_not(present[line]))
        def _(line=line):
            def clear(cell, carry):
                for comp in range(3):
                    wide[line * WIDE + cell, comp] = jnp.zeros((8, 128), F32)
                return carry

            lax.fori_loop(0, WIDE, clear, 0)

    def keep(cell, carry):
        start = pl.multiple_of(((HALF - DEPTH) * half + cell) * 8, 8)
        for comp in range(3):
            wide[own_line * WIDE + DEPTH * other + cell, comp] = spread[comp, pl.ds(start, 8), :]
        return carry

    lax.fori_loop(0, HALF + DEPTH, keep, 0)

    length = 2 * n_blk * HALF

    def reorder(step, carry):
        start = pl.multiple_of(step * 128, 128)
        place = lax.broadcasted_iota(jnp.int32, (128, length), 0) + start
        within = lax.rem(place, length // 2)
        cell = (within // PART) * HALF + (place // (length // 2)) * PART + lax.rem(within, PART)
        hit = cell == lax.broadcasted_iota(jnp.int32, (128, length), 1)
        order[pl.ds(start, 128), :] = jnp.where(hit, 1.0, 0.0).astype(BF16)
        return carry

    lax.fori_loop(0, length // 128, reorder, 0)
    z_copy.wait()

    def turn_z(step, carry):
        start = pl.multiple_of(step * 256, 256)
        z_turned[:, pl.ds(start, 256)] = lax.dot_general(
            order[...], z_mat[pl.ds(start, 256), :], (((1,), (1,)), ((), ())),
            preferred_element_type=F32,
        ).astype(BF16)
        return carry

    lax.fori_loop(0, 4, turn_z, 0)

    def arrive(part, line, low, count):
        pltpu.make_async_copy(
            gathered.at[pl.ds(0, count)], gathered.at[pl.ds(0, count)], gather_recv.at[part, line]
        ).wait()
        per = 2 if count % 2 == 0 else 1

        def some(step, carry):
            for cell in range(per):
                here = line * WIDE + low + step * per + cell
                for comp in range(3):
                    wide[here, comp] = decode(gathered[here, comp])
            return carry

        lax.fori_loop(0, count // per, some, 0)

    lane = lax.broadcasted_iota(jnp.int32, (8, 128), 1)
    last_lane, first_lane = lane == 127, lane == 0

    def advance(source, scale, old, here):
        weight, advect = 0.2 * scale, 0.125 * scale
        center = [source[here, comp] for comp in range(3)]
        pairs = []
        for comp in range(3):
            scaled = center[comp] * advect
            pairs.append((weight - scaled, weight + scaled))
        results = []
        for comp in range(3):
            value = center[comp]
            ahead = pltpu.roll(value, 127, 1)
            ahead = jnp.where(last_lane, pltpu.roll(ahead, 7, 0), ahead)
            behind = pltpu.roll(value, 1, 1)
            behind = jnp.where(first_lane, pltpu.roll(behind, 1, 0), behind)
            total = (pairs[0][0] * ahead + pairs[0][1] * behind) + (
                pairs[1][0] * source[here + WIDE, comp] + pairs[1][1] * source[here - WIDE, comp]
            )
            total = total + (
                pairs[2][0] * source[here + 1, comp] + pairs[2][1] * source[here - 1, comp]
            )
            total = total - weight * value
            if old:
                total = total + old * wide[here, comp]
            results.append(total)
        return results

    def sweep(number, part, d):
        source = (wide, first, second)[number - 1]
        scale, old = ((1.0, None), (0.25, 0.75), (2.0 / 3.0, 1.0 / 3.0))[number - 1]
        low, high = ((d + number, 14 - d - number), (14 - d - number, 22 - d - number))[part]

        def two(step, carry):
            done = []
            for line in (DEPTH - d, DEPTH + 1 + d):
                for cell in range(2):
                    place = low + 2 * step + cell
                    done.append((line, place, advance(source, scale, old, line * WIDE + place)))
            for line, place, results in done:
                for comp in range(3):
                    value = results[comp]
                    if number == 3:
                        start = ((part * 2 + line - DEPTH) * PART + place - low) * 8
                        advanced[comp, pl.ds(pl.multiple_of(start, 8), 8), :] = value
                        continue
                    if d:
                        value = value * inside[line]
                    (first, second)[number - 1][line * WIDE + place, comp] = value
            return carry

        lax.fori_loop(0, (high - low) // 2, two, 0)

    wide_lane = lax.broadcasted_iota(jnp.int32, (2 * PART, 128), 1)
    quarter = wide_lane // 32
    small_quarter = lane // 32
    spot = 2 * blk + half

    def pass_part(part, one, zero):
        for chunk in range(8):
            comps = [
                advanced[comp, pl.ds(part * 128 + chunk, 2 * PART, stride=8), :] for comp in range(3)
            ]
            for number, factors in enumerate(FIELD_FACTORS):
                field = functools.reduce(lambda a, b: a * b, [comps[f] for f in factors])
                rows = slice(number * 2 * PART, (number + 1) * 2 * PART)
                fields[rows, chunk * 128:(chunk + 1) * 128] = (field * zero).astype(BF16)
                fields[rows, 1024 + chunk * 128:1024 + (chunk + 1) * 128] = (field * one).astype(BF16)
        send_ref = (send_first, send_second)[part]
        recv_ref = (recv_first, recv_second)[part]

        def outputs(step, carry):
            dest_grp = lax.rem(grp + 1 + step, n_grp)
            start = pl.multiple_of(dest_grp * n_row * 32, 256)
            contract = (((1,), (1,)), ((), ()))
            passed = lax.dot_general(
                fields[:, 0:1024], x_mat[0, pl.ds(start, 256), :], contract,
                preferred_element_type=F32,
            ) + lax.dot_general(
                fields[:, 1024:2048], x_mat[1, pl.ds(start, 256), :], contract,
                preferred_element_type=F32,
            )
            if part == 0:
                last_low[:, pl.ds(start, 256)] = passed[128:144]
            else:
                lows = last_low[:, pl.ds(start, 256)]
            for tile in range(2):
                lanes = slice(tile * 128, (tile + 1) * 128)
                for four in range(2):
                    turned = []
                    for k in range(4):
                        piece = passed[(four * 4 + k) * 16:(four * 4 + k + 1) * 16, lanes]
                        turned.append(pltpu.roll(piece, 32 * k, 1) if k else piece)
                    for place in range(4):
                        mixed = turned[3]
                        for k in range(3):
                            mixed = jnp.where(quarter == (place + k) % 4, turned[k], mixed)
                        dest = dest_grp * n_row + tile * 4 + place
                        send_ref[dest, four] = mixed[0:PART].astype(BF16)
                        send_ref[n_blk + dest, four] = mixed[PART:2 * PART].astype(BF16)
                if part == 1:
                    for line in range(2):
                        rows = slice(line * PART, (line + 1) * PART)
                        high = pltpu.roll(passed[128:144, lanes][rows], 32, 1)
                        low = lows[rows, lanes]
                        for place in range(4):
                            dest = dest_grp * n_row + tile * 4 + place
                            send_ref[line * n_blk + dest, 2] = jnp.where(
                                small_quarter == place, low, high
                            ).astype(BF16)
            for off in (4, 3, 5, 2, 6, 1, 7, 0):
                dest_row = lax.rem(row + off, n_row)
                dest = dest_grp * n_row + dest_row
                for line in range(2):
                    target = (dest_grp, dest_row, 2 * pln + line)

                    def send(line=line, target=target, dest=dest):
                        pltpu.make_async_remote_copy(
                            src_ref=send_ref.at[line * n_blk + dest], dst_ref=recv_ref.at[spot],
                            send_sem=pass_send.at[part], recv_sem=pass_recv.at[part],
                            device_id=target, device_id_type=MESH,
                        ).start()

                    if off:
                        send()
                    else:
                        pl.when((dest != blk) | (half != line))(send)
            return carry

        lax.fori_loop(0, n_grp, outputs, 0)
        stay = pltpu.make_async_copy(
            send_ref.at[half * n_blk + blk], recv_ref.at[spot], local_sem.at[part]
        )
        stay.start()
        return stay

    stays = []
    for part in range(2):
        for d in range(4):
            if d == 0:
                arrive(part, 4 - half, (0, 14)[part], (14, PART)[part])
                pl.when(half == part)(
                    functools.partial(arrive, part, own_line, (0, DEPTH + HALF)[part], DEPTH)
                )
                continue
            for line in (DEPTH - d, DEPTH + 1 + d):
                pl.when(present[line])(
                    functools.partial(arrive, part, line, (d, 14 - d)[part], (14 - 2 * d, PART)[part])
                )
            for number in range(1, d + 1):
                sweep(number, part, d - number)
        if part == 0:
            pltpu.make_async_copy(
                gathered.at[pl.ds(0, 1)], gathered.at[pl.ds(0, 1)], profile_sem
            ).wait()
            pair_profile = gathered[CELLS, 0].astype(jnp.int32)
            even = jnp.where(half == 0, own_profile, pair_profile).astype(F32)
            odd = jnp.where(half == 0, pair_profile, own_profile).astype(F32)
            one = jnp.concatenate([even, odd], axis=0)
            x_copy.wait()
        stays.append(pass_part(part, one, 1.0 - one))

    contract = (((0,), (0,)), ((), ()))
    many = 2 * n_blk - 1
    middle = length // 2

    def z_filter(cells, rows):
        return lax.dot_general(
            cells.reshape(cells.shape[0] * PART, 128).astype(BF16), z_turned[rows, :], contract,
            preferred_element_type=F32,
        )

    for part, ref in ((0, recv_first), (1, recv_second)):
        stays[part].wait()
        pltpu.make_async_copy(
            ref.at[pl.ds(0, many)], ref.at[pl.ds(0, many)], pass_recv.at[part]
        ).wait()
        rows = slice(part * middle, (part + 1) * middle)
        for four in range(2):
            filtered_part = z_filter(ref[:, four].astype(F32), rows)
            lines = slice(four * 128, (four + 1) * 128)
            if part == 0:
                z_pass[lines, :] = filtered_part
            else:
                z_pass[lines, :] = z_pass[lines, :] + filtered_part
    low = recv_second[:, 2].astype(F32)
    high = pltpu.roll(low.reshape(2 * n_blk * PART, 128), 96, 1).reshape(2 * n_blk, PART, 128)
    z_pass[256:384, :] = z_filter(jnp.concatenate([low, high], axis=0), slice(0, length))

    turn = lax.rem(row, 4)

    def filtered(number):
        start = (number // 4) * 128 + lax.rem(turn + number % 4, 4) * 32
        return z_pass[pl.ds(pl.multiple_of(start, 32), 32), :]

    linear = [filtered(number) for number in range(3)]
    for number, (left, right) in enumerate(PRODUCT_PAIRS):
        direct_ref[number, 0] = filtered(3 + number)
        product_ref[number, 0] = linear[left] * linear[right]

    def sent(sem, count):
        pltpu.make_async_copy(gathered.at[pl.ds(0, count)], gathered.at[pl.ds(0, count)], sem).wait()

    sent(gather_send.at[4], 1)
    sent(gather_send.at[0], 25)
    for d, count in ((1, 40), (2, 36), (3, 32)):
        pl.when(there(pln + steps[d]))(functools.partial(sent, gather_send.at[d], count))
    for part, ref in ((0, send_first), (1, send_second)):
        pltpu.make_async_copy(
            ref.at[pl.ds(0, many)], ref.at[pl.ds(0, many)], pass_send.at[part]
        ).wait()


def solution(mesh):
    sizes = (mesh.shape["grp"], mesh.shape["row"], mesh.shape["col"])
    n_blk = sizes[0] * sizes[1]
    tile = (8, 128)

    def body(velocity, profile, x_filters, z_filter):
        vmem = pl.BlockSpec(memory_space=pltpu.VMEM)
        result = pltpu.VMEM((6, 1, 32, 1024), F32)
        direct, product = pl.pallas_call(
            functools.partial(kernel, sizes),
            out_shape=(result, result),
            in_specs=[
                pl.BlockSpec(memory_space=pltpu.SMEM),
                vmem,
                pl.BlockSpec(memory_space=pl.ANY),
                pl.BlockSpec(memory_space=pl.ANY),
            ],
            out_specs=(vmem, vmem),
            scratch_shapes=[
                pltpu.VMEM((3, 256, 128), F32),
                pltpu.VMEM((2 * HALF + 1, 3) + tile, jnp.int16),
                pltpu.VMEM((CELLS + 1, 3) + tile, jnp.int16),
                pltpu.VMEM((CELLS, 3) + tile, F32),
                pltpu.VMEM((CELLS, 3) + tile, F32),
                pltpu.VMEM((CELLS, 3) + tile, F32),
                pltpu.VMEM((3, 256, 128), F32),
                pltpu.VMEM((9 * 2 * PART, 2048), BF16),
                pltpu.VMEM((2 * PART, 1024), F32),
                pltpu.VMEM((2, 1024, 1024), BF16),
                pltpu.VMEM((1024, 1024), BF16),
                pltpu.VMEM((2 * n_blk, 2) + tile, BF16),
                pltpu.VMEM((2 * n_blk, 3) + tile, BF16),
                pltpu.VMEM((2 * n_blk, 2) + tile, BF16),
                pltpu.VMEM((2 * n_blk, 3) + tile, BF16),
                pltpu.VMEM((384, 1024), F32),
                pltpu.VMEM((1024, 1024), BF16),
                pltpu.VMEM((1024, 1024), BF16),
                pltpu.SemaphoreType.DMA((2,)),
                pltpu.SemaphoreType.DMA((5,)),
                pltpu.SemaphoreType.DMA((2, ROWS)),
                pltpu.SemaphoreType.DMA,
                pltpu.SemaphoreType.DMA((2,)),
                pltpu.SemaphoreType.DMA((2,)),
                pltpu.SemaphoreType.DMA((2,)),
            ],
            compiler_params=pltpu.CompilerParams(
                collective_id=0, has_side_effects=True, vmem_limit_bytes=60000 * 1024
            ),
            name="subgrid",
        )(profile, velocity, x_filters, z_filter)
        return direct - product

    placed = (P(None, "col", ("grp", "row"), None), P("col"), P(), P())
    return jax.shard_map(
        body,
        mesh=mesh,
        in_specs=placed,
        out_specs=P(None, "col", ("grp", "row"), None),
        check_vma=False,
    )
```

```python
import functools

import jax
import jax.numpy as jnp
from jax import lax
from jax.experimental import pallas as pl
from jax.experimental.pallas import tpu as pltpu
from jax.sharding import PartitionSpec as P

F32 = jnp.float32
BF16 = jnp.bfloat16
MESH = pl.DeviceIdType.MESH
PRODUCT_PAIRS = ((0, 0), (0, 1), (0, 2), (1, 1), (1, 2), (2, 2))
FIELD_FACTORS = ((0,), (1,), (2,)) + PRODUCT_PAIRS

DEPTH = 3
HALF = 16
PART = 8
WIDE = HALF + 2 * DEPTH
ROWS = 2 + 2 * DEPTH
CELLS = ROWS * WIDE
CODE_MAX = 32767.0
BOUND = 8.0


def encode(value):
    root = jnp.sqrt(jnp.sqrt(jnp.abs(value) * (1.0 / BOUND)))
    code = (root * CODE_MAX + 0.5).astype(jnp.int32)
    return jnp.where(value < 0.0, -code, code).astype(jnp.int16)


def decode(code):
    root = code.astype(jnp.int32).astype(F32) * (1.0 / CODE_MAX)
    return (root * jnp.abs(root)) * (root * root * BOUND)


def kernel(
    sizes,
    profile_ref, velocity_ref, x_hbm, z_hbm, direct_ref, product_ref,
    spread, coded, gathered, wide, first, second, advanced, fields, last_low,
    x_mat, z_mat, send_first, send_second, recv_first, recv_second, z_pass, order, z_turned,
    weight_sem, gather_send, gather_recv, profile_sem, local_sem, pass_send, pass_recv,
):
    n_grp, n_row, n_col = sizes
    n_blk, n_pln = n_grp * n_row, n_col // 2
    grp, row, col = lax.axis_index("grp"), lax.axis_index("row"), lax.axis_index("col")
    blk = grp * n_row + row
    pln, half = col // 2, col % 2
    other = 1 - half
    toward = 2 * half - 1

    def there(plane):
        return (plane >= 0) & (plane < n_pln)

    grps = [grp] + [
        jnp.where(grp + step < n_grp, grp + step, grp + step - n_grp) for step in range(1, n_grp)
    ]
    rows = [row] + [
        jnp.where(row + step < n_row, row + step, row + step - n_row) for step in range(1, n_row)
    ]
    blocks = {
        0: (grp, row),
        1: (jnp.where(row == n_row - 1, grps[1], grp), rows[1]),
        -1: (jnp.where(row == 0, grps[-1], grp), rows[-1]),
    }
    beside = tuple(
        jnp.where(half == 1, after, before) for before, after in zip(blocks[-1], blocks[1])
    )
    far_first = (4, 3, 5, 2, 6, 1, 7, 0)

    def device(block, plane, side):
        return block + (plane * 2 + side,)

    barrier = pltpu.get_barrier_semaphore()

    def say(target):
        pl.semaphore_signal(barrier, inc=1, device_id=target, device_id_type=MESH)

    for off in far_first:
        for step in range(n_grp):
            for side in (0, 1):
                if off or step:
                    say((grps[step], rows[off], 2 * pln + side))
    say(device(blocks[0], pln, other))
    for step in (-1, 1):
        @pl.when(there(pln + step))
        def _(step=step):
            for side in (0, 1):
                say(device(blocks[0], pln + step, side))
                say(device(beside, pln + step, side))

    @pl.when(there(pln - 2))
    def _():
        say(device(blocks[0], pln - 2, 1))

    @pl.when(there(pln + 2))
    def _():
        say(device(blocks[0], pln + 2, 0))

    x_copy = pltpu.make_async_copy(x_hbm, x_mat, weight_sem.at[0])
    z_copy = pltpu.make_async_copy(z_hbm, z_mat, weight_sem.at[1])
    x_copy.start()
    z_copy.start()

    for group in range(4):
        for comp in range(3):
            for chunk in range(8):
                spread[comp, pl.ds(group * 64 + chunk, 8, stride=8), :] = velocity_ref[
                    comp, 0, group * 8:(group + 1) * 8, chunk * 128:(chunk + 1) * 128
                ]

    def encode_cells(step, carry):
        for cell in range(4):
            start = pl.multiple_of((step * 4 + cell) * 8, 8)
            for comp in range(3):
                coded[step * 4 + cell, comp] = encode(spread[comp, pl.ds(start, 8), :])
        return carry

    lax.fori_loop(0, 2 * HALF // 4, encode_cells, 0)
    own_profile = jnp.full((8, 128), profile_ref[0], jnp.int32)
    for comp in range(3):
        coded[2 * HALF, comp] = own_profile.astype(jnp.int16)

    partners = 2 * n_blk - 1
    for step, count in ((toward, 4), (-toward, 4), (2 * toward, 2)):
        partners = partners + jnp.where(there(pln + step), count, 0)
    pl.semaphore_wait(barrier, partners)

    def give(source, count, cell, part, line, kind, target):
        pltpu.make_async_remote_copy(
            src_ref=coded.at[pl.ds(source, count)],
            dst_ref=gathered.at[pl.ds(line * WIDE + cell, count)],
            send_sem=gather_send.at[kind], recv_sem=gather_recv.at[part, line],
            device_id=target, device_id_type=MESH,
        ).start()

    pltpu.make_async_remote_copy(
        src_ref=coded.at[pl.ds(2 * HALF, 1)], dst_ref=gathered.at[pl.ds(CELLS, 1)],
        send_sem=gather_send.at[4], recv_sem=profile_sem,
        device_id=device(blocks[0], pln, other), device_id_type=MESH,
    ).start()

    own_line = DEPTH + half
    lines = (own_line, 5 - 3 * half, 1 + 5 * half, 7 - 7 * half)
    steps = (0, toward, -toward, 2 * toward)
    for part in range(2):
        for d in range(4):
            def main(side, d=d, part=part):
                target = device(blocks[0], pln + steps[d], side)
                if part == 0 and side == 0:
                    give(0, 11 - d, DEPTH, part, lines[d], d, target)
                elif part == 0:
                    give(13 + d, 14 - 2 * d, d, part, lines[d], d, target)
                elif side == 0:
                    give(11 - d, PART, 14 - d, part, lines[d], d, target)
                else:
                    give(27 - d, 5 + d, 14 - d, part, lines[d], d, target)

            def strip(d=d, part=part):
                if d == 3:
                    return
                if part == 0:
                    give(29 + d, 3 - d, d, part, lines[d], d, device(blocks[1], pln + steps[d], 0))
                else:
                    give(0, 3 - d, DEPTH + HALF, part, lines[d], d, device(blocks[-1], pln + steps[d], 1))

            if d == 0:
                for side in (0, 1):
                    pl.when(half != side)(functools.partial(main, side))
                strip()
            else:
                @pl.when(there(pln + steps[d]))
                def _(main=main, strip=strip):
                    main(0)
                    main(1)
                    strip()

    present = [
        (2 * pln - DEPTH + line >= 0) & (2 * pln - DEPTH + line < n_col) for line in range(ROWS)
    ]
    inside = [jnp.where(known, 1.0, 0.0).astype(F32) for known in present]

    for line in (0, 1, 2, 5, 6, 7):
        @pl.when(jnp.logical_not(present[line]))
        def _(line=line):
            def clear(cell, carry):
                for comp in range(3):
                    wide[line * WIDE + cell, comp] = jnp.zeros((8, 128), F32)
                return carry

            lax.fori_loop(0, WIDE, clear, 0)

    def keep(cell, carry):
        start = pl.multiple_of(((HALF - DEPTH) * half + cell) * 8, 8)
        for comp in range(3):
            wide[own_line * WIDE + DEPTH * other + cell, comp] = spread[comp, pl.ds(start, 8), :]
        return carry

    lax.fori_loop(0, HALF + DEPTH, keep, 0)

    length = 2 * n_blk * HALF

    def reorder(step, carry):
        start = pl.multiple_of(step * 128, 128)
        place = lax.broadcasted_iota(jnp.int32, (128, length), 0) + start
        within = lax.rem(place, length // 2)
        cell = (within // PART) * HALF + (place // (length // 2)) * PART + lax.rem(within, PART)
        hit = cell == lax.broadcasted_iota(jnp.int32, (128, length), 1)
        order[pl.ds(start, 128), :] = jnp.where(hit, 1.0, 0.0).astype(BF16)
        return carry

    lax.fori_loop(0, length // 128, reorder, 0)
    z_copy.wait()

    def turn_z(step, carry):
        start = pl.multiple_of(step * 256, 256)
        z_turned[:, pl.ds(start, 256)] = lax.dot_general(
            order[...], z_mat[pl.ds(start, 256), :], (((1,), (1,)), ((), ())),
            preferred_element_type=F32,
        ).astype(BF16)
        return carry

    lax.fori_loop(0, 4, turn_z, 0)

    def arrive(part, line, low, count):
        pltpu.make_async_copy(
            gathered.at[pl.ds(0, count)], gathered.at[pl.ds(0, count)], gather_recv.at[part, line]
        ).wait()
        per = 2 if count % 2 == 0 else 1

        def some(step, carry):
            for cell in range(per):
                here = line * WIDE + low + step * per + cell
                for comp in range(3):
                    wide[here, comp] = decode(gathered[here, comp])
            return carry

        lax.fori_loop(0, count // per, some, 0)

    lane = lax.broadcasted_iota(jnp.int32, (8, 128), 1)
    last_lane, first_lane = lane == 127, lane == 0

    def advance(source, scale, old, here):
        weight, advect = 0.2 * scale, 0.125 * scale
        center = [source[here, comp] for comp in range(3)]
        pairs = []
        for comp in range(3):
            scaled = center[comp] * advect
            pairs.append((weight - scaled, weight + scaled))
        results = []
        for comp in range(3):
            value = center[comp]
            ahead = pltpu.roll(value, 127, 1)
            ahead = jnp.where(last_lane, pltpu.roll(ahead, 7, 0), ahead)
            behind = pltpu.roll(value, 1, 1)
            behind = jnp.where(first_lane, pltpu.roll(behind, 1, 0), behind)
            total = (pairs[0][0] * ahead + pairs[0][1] * behind) + (
                pairs[1][0] * source[here + WIDE, comp] + pairs[1][1] * source[here - WIDE, comp]
            )
            total = total + (
                pairs[2][0] * source[here + 1, comp] + pairs[2][1] * source[here - 1, comp]
            )
            total = total - weight * value
            if old:
                total = total + old * wide[here, comp]
            results.append(total)
        return results

    def sweep(number, part, d):
        source = (wide, first, second)[number - 1]
        scale, old = ((1.0, None), (0.25, 0.75), (2.0 / 3.0, 1.0 / 3.0))[number - 1]
        low, high = ((d + number, 14 - d - number), (14 - d - number, 22 - d - number))[part]

        def two(step, carry):
            done = []
            for line in (DEPTH - d, DEPTH + 1 + d):
                for cell in range(2):
                    place = low + 2 * step + cell
                    done.append((line, place, advance(source, scale, old, line * WIDE + place)))
            for line, place, results in done:
                for comp in range(3):
                    value = results[comp]
                    if number == 3:
                        start = ((part * 2 + line - DEPTH) * PART + place - low) * 8
                        advanced[comp, pl.ds(pl.multiple_of(start, 8), 8), :] = value
                        continue
                    if d:
                        value = value * inside[line]
                    (first, second)[number - 1][line * WIDE + place, comp] = value
            return carry

        lax.fori_loop(0, (high - low) // 2, two, 0)

    wide_lane = lax.broadcasted_iota(jnp.int32, (2 * PART, 128), 1)
    quarter = wide_lane // 32
    small_quarter = lane // 32
    spot = 2 * blk + half

    def pass_part(part, one, zero):
        for chunk in range(8):
            comps = [
                advanced[comp, pl.ds(part * 128 + chunk, 2 * PART, stride=8), :] for comp in range(3)
            ]
            for number, factors in enumerate(FIELD_FACTORS):
                field = functools.reduce(lambda a, b: a * b, [comps[f] for f in factors])
                lines = slice(number * 2 * PART, (number + 1) * 2 * PART)
                fields[lines, chunk * 128:(chunk + 1) * 128] = (field * zero).astype(BF16)
                fields[lines, 1024 + chunk * 128:1024 + (chunk + 1) * 128] = (field * one).astype(BF16)
        send_ref = (send_first, send_second)[part]
        recv_ref = (recv_first, recv_second)[part]

        def outputs(step, carry):
            dest_grp = lax.rem(grp + 1 + step, n_grp)
            start = pl.multiple_of(dest_grp * n_row * 32, 256)
            contract = (((1,), (1,)), ((), ()))
            passed = lax.dot_general(
                fields[:, 0:1024], x_mat[0, pl.ds(start, 256), :], contract,
                preferred_element_type=F32,
            ) + lax.dot_general(
                fields[:, 1024:2048], x_mat[1, pl.ds(start, 256), :], contract,
                preferred_element_type=F32,
            )
            if part == 0:
                last_low[:, pl.ds(start, 256)] = passed[128:144]
            else:
                lows = last_low[:, pl.ds(start, 256)]
            for tile in range(2):
                lanes = slice(tile * 128, (tile + 1) * 128)
                for four in range(2):
                    turned = []
                    for k in range(4):
                        piece = passed[(four * 4 + k) * 16:(four * 4 + k + 1) * 16, lanes]
                        turned.append(pltpu.roll(piece, 32 * k, 1) if k else piece)
                    for place in range(4):
                        mixed = turned[3]
                        for k in range(3):
                            mixed = jnp.where(quarter == (place + k) % 4, turned[k], mixed)
                        dest = dest_grp * n_row + tile * 4 + place
                        send_ref[dest, four] = mixed[0:PART].astype(BF16)
                        send_ref[n_blk + dest, four] = mixed[PART:2 * PART].astype(BF16)
                if part == 1:
                    for line in range(2):
                        band = slice(line * PART, (line + 1) * PART)
                        high = pltpu.roll(passed[128:144, lanes][band], 32, 1)
                        low = lows[band, lanes]
                        for place in range(4):
                            dest = dest_grp * n_row + tile * 4 + place
                            send_ref[line * n_blk + dest, 2] = jnp.where(
                                small_quarter == place, low, high
                            ).astype(BF16)
            for off in far_first:
                dest_row = rows[off]
                dest = dest_grp * n_row + dest_row
                for line in range(2):
                    target = (dest_grp, dest_row, 2 * pln + line)

                    def send(line=line, target=target, dest=dest):
                        pltpu.make_async_remote_copy(
                            src_ref=send_ref.at[line * n_blk + dest], dst_ref=recv_ref.at[spot],
                            send_sem=pass_send.at[part], recv_sem=pass_recv.at[part],
                            device_id=target, device_id_type=MESH,
                        ).start()

                    if off:
                        send()
                    else:
                        pl.when((dest != blk) | (half != line))(send)
            return carry

        lax.fori_loop(0, n_grp, outputs, 0)
        stay = pltpu.make_async_copy(
            send_ref.at[half * n_blk + blk], recv_ref.at[spot], local_sem.at[part]
        )
        stay.start()
        return stay

    stays = []
    for part in range(2):
        for d in range(4):
            if d == 0:
                arrive(part, 4 - half, (0, 14)[part], (14, PART)[part])
                pl.when(half == part)(
                    functools.partial(arrive, part, own_line, (0, DEPTH + HALF)[part], DEPTH)
                )
                continue
            for line in (DEPTH - d, DEPTH + 1 + d):
                pl.when(present[line])(
                    functools.partial(arrive, part, line, (d, 14 - d)[part], (14 - 2 * d, PART)[part])
                )
            for number in range(1, d + 1):
                sweep(number, part, d - number)
        if part == 0:
            pltpu.make_async_copy(
                gathered.at[pl.ds(0, 1)], gathered.at[pl.ds(0, 1)], profile_sem
            ).wait()
            pair_profile = gathered[CELLS, 0].astype(jnp.int32)
            even = jnp.where(half == 0, own_profile, pair_profile).astype(F32)
            odd = jnp.where(half == 0, pair_profile, own_profile).astype(F32)
            one = jnp.concatenate([even, odd], axis=0)
            x_copy.wait()
        stays.append(pass_part(part, one, 1.0 - one))

    contract = (((0,), (0,)), ((), ()))
    many = 2 * n_blk - 1
    middle = length // 2

    def z_filter(cells, rows):
        return lax.dot_general(
            cells.reshape(cells.shape[0] * PART, 128).astype(BF16), z_turned[rows, :], contract,
            preferred_element_type=F32,
        )

    for part, ref in ((0, recv_first), (1, recv_second)):
        stays[part].wait()
        pltpu.make_async_copy(
            ref.at[pl.ds(0, many)], ref.at[pl.ds(0, many)], pass_recv.at[part]
        ).wait()
        cells = slice(part * middle, (part + 1) * middle)
        for four in range(2):
            filtered_part = z_filter(ref[:, four].astype(F32), cells)
            lines = slice(four * 128, (four + 1) * 128)
            if part == 0:
                z_pass[lines, :] = filtered_part
            else:
                z_pass[lines, :] = z_pass[lines, :] + filtered_part
    low = recv_second[:, 2].astype(F32)
    high = pltpu.roll(low.reshape(2 * n_blk * PART, 128), 96, 1).reshape(2 * n_blk, PART, 128)
    z_pass[256:384, :] = z_filter(jnp.concatenate([low, high], axis=0), slice(0, length))

    turn = lax.rem(row, 4)

    def filtered(number):
        start = (number // 4) * 128 + lax.rem(turn + number % 4, 4) * 32
        return z_pass[pl.ds(pl.multiple_of(start, 32), 32), :]

    linear = [filtered(number) for number in range(3)]
    for number, (left, right) in enumerate(PRODUCT_PAIRS):
        direct_ref[number, 0] = filtered(3 + number)
        product_ref[number, 0] = linear[left] * linear[right]

    def sent(sem, count):
        pltpu.make_async_copy(gathered.at[pl.ds(0, count)], gathered.at[pl.ds(0, count)], sem).wait()

    sent(gather_send.at[4], 1)
    sent(gather_send.at[0], 25)
    for d, count in ((1, 40), (2, 36), (3, 32)):
        pl.when(there(pln + steps[d]))(functools.partial(sent, gather_send.at[d], count))
    for part, ref in ((0, send_first), (1, send_second)):
        pltpu.make_async_copy(
            ref.at[pl.ds(0, many)], ref.at[pl.ds(0, many)], pass_send.at[part]
        ).wait()


def solution(mesh):
    sizes = (mesh.shape["grp"], mesh.shape["row"], mesh.shape["col"])
    n_blk = sizes[0] * sizes[1]
    tile = (8, 128)

    def body(velocity, profile, x_filters, z_filter):
        vmem = pl.BlockSpec(memory_space=pltpu.VMEM)
        result = pltpu.VMEM((6, 1, 32, 1024), F32)
        direct, product = pl.pallas_call(
            functools.partial(kernel, sizes),
            out_shape=(result, result),
            in_specs=[
                pl.BlockSpec(memory_space=pltpu.SMEM),
                vmem,
                pl.BlockSpec(memory_space=pl.ANY),
                pl.BlockSpec(memory_space=pl.ANY),
            ],
            out_specs=(vmem, vmem),
            scratch_shapes=[
                pltpu.VMEM((3, 256, 128), F32),
                pltpu.VMEM((2 * HALF + 1, 3) + tile, jnp.int16),
                pltpu.VMEM((CELLS + 1, 3) + tile, jnp.int16),
                pltpu.VMEM((CELLS, 3) + tile, F32),
                pltpu.VMEM((CELLS, 3) + tile, F32),
                pltpu.VMEM((CELLS, 3) + tile, F32),
                pltpu.VMEM((3, 256, 128), F32),
                pltpu.VMEM((9 * 2 * PART, 2048), BF16),
                pltpu.VMEM((2 * PART, 1024), F32),
                pltpu.VMEM((2, 1024, 1024), BF16),
                pltpu.VMEM((1024, 1024), BF16),
                pltpu.VMEM((2 * n_blk, 2) + tile, BF16),
                pltpu.VMEM((2 * n_blk, 3) + tile, BF16),
                pltpu.VMEM((2 * n_blk, 2) + tile, BF16),
                pltpu.VMEM((2 * n_blk, 3) + tile, BF16),
                pltpu.VMEM((384, 1024), F32),
                pltpu.VMEM((1024, 1024), BF16),
                pltpu.VMEM((1024, 1024), BF16),
                pltpu.SemaphoreType.DMA((2,)),
                pltpu.SemaphoreType.DMA((5,)),
                pltpu.SemaphoreType.DMA((2, ROWS)),
                pltpu.SemaphoreType.DMA,
                pltpu.SemaphoreType.DMA((2,)),
                pltpu.SemaphoreType.DMA((2,)),
                pltpu.SemaphoreType.DMA((2,)),
            ],
            compiler_params=pltpu.CompilerParams(
                collective_id=0, has_side_effects=True, vmem_limit_bytes=60000 * 1024
            ),
            name="subgrid",
        )(profile, velocity, x_filters, z_filter)
        return direct - product

    placed = (P(None, "col", ("grp", "row"), None), P("col"), P(), P())
    return jax.shard_map(
        body,
        mesh=mesh,
        in_specs=placed,
        out_specs=P(None, "col", ("grp", "row"), None),
        check_vma=False,
    )
```

```python
import functools

import jax
import jax.numpy as jnp
from jax import lax
from jax.experimental import pallas as pl
from jax.experimental.pallas import tpu as pltpu
from jax.sharding import PartitionSpec as P

F32 = jnp.float32
BF16 = jnp.bfloat16
MESH = pl.DeviceIdType.MESH
PRODUCT_PAIRS = ((0, 0), (0, 1), (0, 2), (1, 1), (1, 2), (2, 2))
FIELD_FACTORS = ((0,), (1,), (2,)) + PRODUCT_PAIRS

DEPTH = 3
HALF = 16
PART = 8
WIDE = HALF + 2 * DEPTH
ROWS = 2 + 2 * DEPTH
CELLS = ROWS * WIDE
CODE_MAX = 32767.0
BOUND = 8.0


def encode(value):
    root = jnp.sqrt(jnp.sqrt(jnp.abs(value) * (1.0 / BOUND)))
    code = (root * CODE_MAX + 0.5).astype(jnp.int32)
    return jnp.where(value < 0.0, -code, code).astype(jnp.int16)


def decode(code):
    root = code.astype(jnp.int32).astype(F32) * (1.0 / CODE_MAX)
    return (root * jnp.abs(root)) * (root * root * BOUND)


def kernel(
    sizes,
    profile_ref, velocity_ref, x_hbm, z_hbm, direct_ref, product_ref,
    spread, coded, gathered, wide, first, second, advanced, fields, last_low,
    x_mat, z_mat, send_first, send_second, recv_first, recv_second, z_pass, order, z_turned,
    weight_sem, gather_send, gather_recv, profile_sem, local_sem, pass_send, pass_recv,
):
    n_grp, n_row, n_col = sizes
    n_blk, n_pln = n_grp * n_row, n_col // 2
    grp, row, col = lax.axis_index("grp"), lax.axis_index("row"), lax.axis_index("col")
    blk = grp * n_row + row
    pln, half = col // 2, col % 2
    other = 1 - half
    toward = 2 * half - 1

    def there(plane):
        return (plane >= 0) & (plane < n_pln)

    grps = [grp] + [
        jnp.where(grp + step < n_grp, grp + step, grp + step - n_grp) for step in range(1, n_grp)
    ]
    rows = [row] + [
        jnp.where(row + step < n_row, row + step, row + step - n_row) for step in range(1, n_row)
    ]
    blocks = {
        0: (grp, row),
        1: (jnp.where(row == n_row - 1, grps[1], grp), rows[1]),
        -1: (jnp.where(row == 0, grps[-1], grp), rows[-1]),
    }
    beside = tuple(
        jnp.where(half == 1, after, before) for before, after in zip(blocks[-1], blocks[1])
    )
    far_first = (4, 3, 5, 2, 6, 1, 7, 0)

    def device(block, plane, side):
        return block + (plane * 2 + side,)

    barrier = pltpu.get_barrier_semaphore()

    def say(target):
        pl.semaphore_signal(barrier, inc=1, device_id=target, device_id_type=MESH)

    for off in far_first:
        for step in range(n_grp):
            for side in (0, 1):
                if off or step:
                    say((grps[step], rows[off], 2 * pln + side))
    say(device(blocks[0], pln, other))
    for step in (-1, 1):
        @pl.when(there(pln + step))
        def _(step=step):
            for side in (0, 1):
                say(device(blocks[0], pln + step, side))
                say(device(beside, pln + step, side))

    @pl.when(there(pln - 2))
    def _():
        say(device(blocks[0], pln - 2, 1))

    @pl.when(there(pln + 2))
    def _():
        say(device(blocks[0], pln + 2, 0))

    x_copy = pltpu.make_async_copy(x_hbm, x_mat, weight_sem.at[0])
    z_copy = pltpu.make_async_copy(z_hbm, z_mat, weight_sem.at[1])
    x_copy.start()
    z_copy.start()

    for group in range(4):
        for comp in range(3):
            for chunk in range(8):
                spread[comp, pl.ds(group * 64 + chunk, 8, stride=8), :] = velocity_ref[
                    comp, 0, group * 8:(group + 1) * 8, chunk * 128:(chunk + 1) * 128
                ]

    def encode_cells(step, carry):
        for cell in range(4):
            start = pl.multiple_of((step * 4 + cell) * 8, 8)
            for comp in range(3):
                coded[step * 4 + cell, comp] = encode(spread[comp, pl.ds(start, 8), :])
        return carry

    lax.fori_loop(0, 2 * HALF // 4, encode_cells, 0)
    own_profile = jnp.full((8, 128), profile_ref[0], jnp.int32)
    for comp in range(3):
        coded[2 * HALF, comp] = own_profile.astype(jnp.int16)

    partners = 2 * n_blk - 1
    for step, count in ((toward, 4), (-toward, 4), (2 * toward, 2)):
        partners = partners + jnp.where(there(pln + step), count, 0)
    pl.semaphore_wait(barrier, partners)

    def give(source, count, cell, part, line, kind, target):
        pltpu.make_async_remote_copy(
            src_ref=coded.at[pl.ds(source, count)],
            dst_ref=gathered.at[pl.ds(line * WIDE + cell, count)],
            send_sem=gather_send.at[kind], recv_sem=gather_recv.at[part, line],
            device_id=target, device_id_type=MESH,
        ).start()

    pltpu.make_async_remote_copy(
        src_ref=coded.at[pl.ds(2 * HALF, 1)], dst_ref=gathered.at[pl.ds(CELLS, 1)],
        send_sem=gather_send.at[4], recv_sem=profile_sem,
        device_id=device(blocks[0], pln, other), device_id_type=MESH,
    ).start()

    own_line = DEPTH + half
    lines = (own_line, 5 - 3 * half, 1 + 5 * half, 7 - 7 * half)
    steps = (0, toward, -toward, 2 * toward)
    for part in range(2):
        for d in range(4):
            def main(side, d=d, part=part):
                target = device(blocks[0], pln + steps[d], side)
                if part == 0 and side == 0:
                    give(0, 11 - d, DEPTH, part, lines[d], d, target)
                elif part == 0:
                    give(13 + d, 14 - 2 * d, d, part, lines[d], d, target)
                elif side == 0:
                    give(11 - d, PART, 14 - d, part, lines[d], d, target)
                else:
                    give(27 - d, 5 + d, 14 - d, part, lines[d], d, target)

            def strip(d=d, part=part):
                if d == 3:
                    return
                if part == 0:
                    give(29 + d, 3 - d, d, part, lines[d], d, device(blocks[1], pln + steps[d], 0))
                else:
                    give(0, 3 - d, DEPTH + HALF, part, lines[d], d, device(blocks[-1], pln + steps[d], 1))

            if d == 0:
                for side in (0, 1):
                    pl.when(half != side)(functools.partial(main, side))
                strip()
            else:
                @pl.when(there(pln + steps[d]))
                def _(main=main, strip=strip):
                    main(0)
                    main(1)
                    strip()

    present = [
        (2 * pln - DEPTH + line >= 0) & (2 * pln - DEPTH + line < n_col) for line in range(ROWS)
    ]
    inside = [jnp.where(known, 1.0, 0.0).astype(F32) for known in present]

    for line in (0, 1, 2, 5, 6, 7):
        @pl.when(jnp.logical_not(present[line]))
        def _(line=line):
            def clear(cell, carry):
                for comp in range(3):
                    wide[line * WIDE + cell, comp] = jnp.zeros((8, 128), F32)
                return carry

            lax.fori_loop(0, WIDE, clear, 0)

    def keep(cell, carry):
        start = pl.multiple_of(((HALF - DEPTH) * half + cell) * 8, 8)
        for comp in range(3):
            wide[own_line * WIDE + DEPTH * other + cell, comp] = spread[comp, pl.ds(start, 8), :]
        return carry

    lax.fori_loop(0, HALF + DEPTH, keep, 0)

    length = 2 * n_blk * HALF

    def reorder(step, carry):
        start = pl.multiple_of(step * 128, 128)
        place = lax.broadcasted_iota(jnp.int32, (128, length), 0) + start
        within = lax.rem(place, length // 2)
        cell = (within // PART) * HALF + (place // (length // 2)) * PART + lax.rem(within, PART)
        hit = cell == lax.broadcasted_iota(jnp.int32, (128, length), 1)
        order[pl.ds(start, 128), :] = jnp.where(hit, 1.0, 0.0).astype(BF16)
        return carry

    lax.fori_loop(0, length // 128, reorder, 0)
    z_copy.wait()

    def turn_z(step, carry):
        start = pl.multiple_of(step * 256, 256)
        z_turned[:, pl.ds(start, 256)] = lax.dot_general(
            order[...], z_mat[pl.ds(start, 256), :], (((1,), (1,)), ((), ())),
            preferred_element_type=F32,
        ).astype(BF16)
        return carry

    lax.fori_loop(0, 4, turn_z, 0)

    def arrive(part, line, low, count):
        pltpu.make_async_copy(
            gathered.at[pl.ds(0, count)], gathered.at[pl.ds(0, count)], gather_recv.at[part, line]
        ).wait()
        per = count // 2 if count % 2 == 0 else count

        def some(step, carry):
            for cell in range(per):
                here = line * WIDE + low + step * per + cell
                for comp in range(3):
                    wide[here, comp] = decode(gathered[here, comp])
            return carry

        lax.fori_loop(0, count // per, some, 0)

    lane = lax.broadcasted_iota(jnp.int32, (8, 128), 1)
    last_lane, first_lane = lane == 127, lane == 0

    def advance(source, scale, old, here):
        weight, advect = 0.2 * scale, 0.125 * scale
        center = [source[here, comp] for comp in range(3)]
        pairs = []
        for comp in range(3):
            scaled = center[comp] * advect
            pairs.append((weight - scaled, weight + scaled))
        results = []
        for comp in range(3):
            value = center[comp]
            ahead = pltpu.roll(value, 127, 1)
            ahead = jnp.where(last_lane, pltpu.roll(ahead, 7, 0), ahead)
            behind = pltpu.roll(value, 1, 1)
            behind = jnp.where(first_lane, pltpu.roll(behind, 1, 0), behind)
            total = (pairs[0][0] * ahead + pairs[0][1] * behind) + (
                pairs[1][0] * source[here + WIDE, comp] + pairs[1][1] * source[here - WIDE, comp]
            )
            total = total + (
                pairs[2][0] * source[here + 1, comp] + pairs[2][1] * source[here - 1, comp]
            )
            total = total - weight * value
            if old:
                total = total + old * wide[here, comp]
            results.append(total)
        return results

    def sweep(number, part, d):
        source = (wide, first, second)[number - 1]
        scale, old = ((1.0, None), (0.25, 0.75), (2.0 / 3.0, 1.0 / 3.0))[number - 1]
        low, high = ((d + number, 14 - d - number), (14 - d - number, 22 - d - number))[part]

        per = 5 if (high - low) % 4 else 4

        def some(step, carry):
            done = []
            for line in (DEPTH - d, DEPTH + 1 + d):
                for cell in range(per):
                    place = low + per * step + cell
                    done.append((line, place, advance(source, scale, old, line * WIDE + place)))
            for line, place, results in done:
                for comp in range(3):
                    value = results[comp]
                    if number == 3:
                        start = ((part * 2 + line - DEPTH) * PART + place - low) * 8
                        advanced[comp, pl.ds(pl.multiple_of(start, 8), 8), :] = value
                        continue
                    if d:
                        value = value * inside[line]
                    (first, second)[number - 1][line * WIDE + place, comp] = value
            return carry

        lax.fori_loop(0, (high - low) // per, some, 0)

    wide_lane = lax.broadcasted_iota(jnp.int32, (2 * PART, 128), 1)
    quarter = wide_lane // 32
    small_quarter = lane // 32
    spot = 2 * blk + half

    def pass_part(part, one, zero):
        for chunk in range(8):
            comps = [
                advanced[comp, pl.ds(part * 128 + chunk, 2 * PART, stride=8), :] for comp in range(3)
            ]
            for number, factors in enumerate(FIELD_FACTORS):
                field = functools.reduce(lambda a, b: a * b, [comps[f] for f in factors])
                lines = slice(number * 2 * PART, (number + 1) * 2 * PART)
                fields[lines, chunk * 128:(chunk + 1) * 128] = (field * zero).astype(BF16)
                fields[lines, 1024 + chunk * 128:1024 + (chunk + 1) * 128] = (field * one).astype(BF16)
        send_ref = (send_first, send_second)[part]
        recv_ref = (recv_first, recv_second)[part]

        def outputs(step, carry):
            dest_grp = lax.rem(grp + 1 + step, n_grp)
            start = pl.multiple_of(dest_grp * n_row * 32, 256)
            contract = (((1,), (1,)), ((), ()))
            passed = lax.dot_general(
                fields[:, 0:1024], x_mat[0, pl.ds(start, 256), :], contract,
                preferred_element_type=F32,
            ) + lax.dot_general(
                fields[:, 1024:2048], x_mat[1, pl.ds(start, 256), :], contract,
                preferred_element_type=F32,
            )
            if part == 0:
                last_low[:, pl.ds(start, 256)] = passed[128:144]
            else:
                lows = last_low[:, pl.ds(start, 256)]
            for tile in range(2):
                lanes = slice(tile * 128, (tile + 1) * 128)
                for four in range(2):
                    turned = []
                    for k in range(4):
                        piece = passed[(four * 4 + k) * 16:(four * 4 + k + 1) * 16, lanes]
                        turned.append(pltpu.roll(piece, 32 * k, 1) if k else piece)
                    for place in range(4):
                        mixed = turned[3]
                        for k in range(3):
                            mixed = jnp.where(quarter == (place + k) % 4, turned[k], mixed)
                        dest = dest_grp * n_row + tile * 4 + place
                        send_ref[dest, four] = mixed[0:PART].astype(BF16)
                        send_ref[n_blk + dest, four] = mixed[PART:2 * PART].astype(BF16)
                if part == 1:
                    for line in range(2):
                        band = slice(line * PART, (line + 1) * PART)
                        high = pltpu.roll(passed[128:144, lanes][band], 32, 1)
                        low = lows[band, lanes]
                        for place in range(4):
                            dest = dest_grp * n_row + tile * 4 + place
                            send_ref[line * n_blk + dest, 2] = jnp.where(
                                small_quarter == place, low, high
                            ).astype(BF16)
            for off in far_first:
                dest_row = rows[off]
                dest = dest_grp * n_row + dest_row
                for line in range(2):
                    target = (dest_grp, dest_row, 2 * pln + line)

                    def send(line=line, target=target, dest=dest):
                        pltpu.make_async_remote_copy(
                            src_ref=send_ref.at[line * n_blk + dest], dst_ref=recv_ref.at[spot],
                            send_sem=pass_send.at[part], recv_sem=pass_recv.at[part],
                            device_id=target, device_id_type=MESH,
                        ).start()

                    if off:
                        send()
                    else:
                        pl.when((dest != blk) | (half != line))(send)
            return carry

        lax.fori_loop(0, n_grp, outputs, 0)
        stay = pltpu.make_async_copy(
            send_ref.at[half * n_blk + blk], recv_ref.at[spot], local_sem.at[part]
        )
        stay.start()
        return stay

    stays = []
    for part in range(2):
        for d in range(4):
            if d == 0:
                arrive(part, 4 - half, (0, 14)[part], (14, PART)[part])
                pl.when(half == part)(
                    functools.partial(arrive, part, own_line, (0, DEPTH + HALF)[part], DEPTH)
                )
                continue
            for line in (DEPTH - d, DEPTH + 1 + d):
                pl.when(present[line])(
                    functools.partial(arrive, part, line, (d, 14 - d)[part], (14 - 2 * d, PART)[part])
                )
            for number in range(1, d + 1):
                sweep(number, part, d - number)
        if part == 0:
            pltpu.make_async_copy(
                gathered.at[pl.ds(0, 1)], gathered.at[pl.ds(0, 1)], profile_sem
            ).wait()
            pair_profile = gathered[CELLS, 0].astype(jnp.int32)
            even = jnp.where(half == 0, own_profile, pair_profile).astype(F32)
            odd = jnp.where(half == 0, pair_profile, own_profile).astype(F32)
            one = jnp.concatenate([even, odd], axis=0)
            x_copy.wait()
        stays.append(pass_part(part, one, 1.0 - one))

    contract = (((0,), (0,)), ((), ()))
    many = 2 * n_blk - 1
    middle = length // 2

    def z_filter(cells, rows):
        return lax.dot_general(
            cells.reshape(cells.shape[0] * PART, 128).astype(BF16), z_turned[rows, :], contract,
            preferred_element_type=F32,
        )

    for part, ref in ((0, recv_first), (1, recv_second)):
        stays[part].wait()
        pltpu.make_async_copy(
            ref.at[pl.ds(0, many)], ref.at[pl.ds(0, many)], pass_recv.at[part]
        ).wait()
        cells = slice(part * middle, (part + 1) * middle)
        for four in range(2):
            filtered_part = z_filter(ref[:, four].astype(F32), cells)
            lines = slice(four * 128, (four + 1) * 128)
            if part == 0:
                z_pass[lines, :] = filtered_part
            else:
                z_pass[lines, :] = z_pass[lines, :] + filtered_part
    low = recv_second[:, 2].astype(F32)
    high = pltpu.roll(low.reshape(2 * n_blk * PART, 128), 96, 1).reshape(2 * n_blk, PART, 128)
    z_pass[256:384, :] = z_filter(jnp.concatenate([low, high], axis=0), slice(0, length))

    turn = lax.rem(row, 4)

    def filtered(number):
        start = (number // 4) * 128 + lax.rem(turn + number % 4, 4) * 32
        return z_pass[pl.ds(pl.multiple_of(start, 32), 32), :]

    linear = [filtered(number) for number in range(3)]
    for number, (left, right) in enumerate(PRODUCT_PAIRS):
        direct_ref[number, 0] = filtered(3 + number)
        product_ref[number, 0] = linear[left] * linear[right]

    def sent(sem, count):
        pltpu.make_async_copy(gathered.at[pl.ds(0, count)], gathered.at[pl.ds(0, count)], sem).wait()

    sent(gather_send.at[4], 1)
    sent(gather_send.at[0], 25)
    for d, count in ((1, 40), (2, 36), (3, 32)):
        pl.when(there(pln + steps[d]))(functools.partial(sent, gather_send.at[d], count))
    for part, ref in ((0, send_first), (1, send_second)):
        pltpu.make_async_copy(
            ref.at[pl.ds(0, many)], ref.at[pl.ds(0, many)], pass_send.at[part]
        ).wait()


def solution(mesh):
    sizes = (mesh.shape["grp"], mesh.shape["row"], mesh.shape["col"])
    n_blk = sizes[0] * sizes[1]
    tile = (8, 128)

    def body(velocity, profile, x_filters, z_filter):
        vmem = pl.BlockSpec(memory_space=pltpu.VMEM)
        result = pltpu.VMEM((6, 1, 32, 1024), F32)
        direct, product = pl.pallas_call(
            functools.partial(kernel, sizes),
            out_shape=(result, result),
            in_specs=[
                pl.BlockSpec(memory_space=pltpu.SMEM),
                vmem,
                pl.BlockSpec(memory_space=pl.ANY),
                pl.BlockSpec(memory_space=pl.ANY),
            ],
            out_specs=(vmem, vmem),
            scratch_shapes=[
                pltpu.VMEM((3, 256, 128), F32),
                pltpu.VMEM((2 * HALF + 1, 3) + tile, jnp.int16),
                pltpu.VMEM((CELLS + 1, 3) + tile, jnp.int16),
                pltpu.VMEM((CELLS, 3) + tile, F32),
                pltpu.VMEM((CELLS, 3) + tile, F32),
                pltpu.VMEM((CELLS, 3) + tile, F32),
                pltpu.VMEM((3, 256, 128), F32),
                pltpu.VMEM((9 * 2 * PART, 2048), BF16),
                pltpu.VMEM((2 * PART, 1024), F32),
                pltpu.VMEM((2, 1024, 1024), BF16),
                pltpu.VMEM((1024, 1024), BF16),
                pltpu.VMEM((2 * n_blk, 2) + tile, BF16),
                pltpu.VMEM((2 * n_blk, 3) + tile, BF16),
                pltpu.VMEM((2 * n_blk, 2) + tile, BF16),
                pltpu.VMEM((2 * n_blk, 3) + tile, BF16),
                pltpu.VMEM((384, 1024), F32),
                pltpu.VMEM((1024, 1024), BF16),
                pltpu.VMEM((1024, 1024), BF16),
                pltpu.SemaphoreType.DMA((2,)),
                pltpu.SemaphoreType.DMA((5,)),
                pltpu.SemaphoreType.DMA((2, ROWS)),
                pltpu.SemaphoreType.DMA,
                pltpu.SemaphoreType.DMA((2,)),
                pltpu.SemaphoreType.DMA((2,)),
                pltpu.SemaphoreType.DMA((2,)),
            ],
            compiler_params=pltpu.CompilerParams(
                collective_id=0, has_side_effects=True, vmem_limit_bytes=60000 * 1024
            ),
            name="subgrid",
        )(profile, velocity, x_filters, z_filter)
        return direct - product

    placed = (P(None, "col", ("grp", "row"), None), P("col"), P(), P())
    return jax.shard_map(
        body,
        mesh=mesh,
        in_specs=placed,
        out_specs=P(None, "col", ("grp", "row"), None),
        check_vma=False,
    )
```

```python
import functools

import jax
import jax.numpy as jnp
from jax import lax
from jax.experimental import pallas as pl
from jax.experimental.pallas import tpu as pltpu
from jax.sharding import PartitionSpec as P

F32 = jnp.float32
BF16 = jnp.bfloat16
MESH = pl.DeviceIdType.MESH
PRODUCT_PAIRS = ((0, 0), (0, 1), (0, 2), (1, 1), (1, 2), (2, 2))
FIELD_FACTORS = ((0,), (1,), (2,)) + PRODUCT_PAIRS

DEPTH = 3
HALF = 16
PART = 8
WIDE = HALF + 2 * DEPTH
ROWS = 2 + 2 * DEPTH
CELLS = ROWS * WIDE
CODE_MAX = 32767.0
BOUND = 8.0


def encode(value):
    root = jnp.sqrt(jnp.sqrt(jnp.abs(value) * (1.0 / BOUND)))
    code = (root * CODE_MAX + 0.5).astype(jnp.int32)
    return jnp.where(value < 0.0, -code, code).astype(jnp.int16)


def decode(code):
    root = code.astype(jnp.int32).astype(F32) * (1.0 / CODE_MAX)
    return (root * jnp.abs(root)) * (root * root * BOUND)


def kernel(
    sizes,
    profile_ref, velocity_ref, x_hbm, z_hbm, direct_ref, product_ref,
    spread, coded, gathered, wide, first, second, advanced, fields, last_low,
    x_mat, z_mat, send_first, send_second, recv_first, recv_second, z_pass, order, z_turned,
    weight_sem, gather_send, gather_recv, profile_sem, local_sem, pass_send, pass_recv,
):
    n_grp, n_row, n_col = sizes
    n_blk, n_pln = n_grp * n_row, n_col // 2
    grp, row, col = lax.axis_index("grp"), lax.axis_index("row"), lax.axis_index("col")
    blk = grp * n_row + row
    pln, half = col // 2, col % 2
    other = 1 - half
    toward = 2 * half - 1

    def there(plane):
        return (plane >= 0) & (plane < n_pln)

    grps = [grp] + [
        jnp.where(grp + step < n_grp, grp + step, grp + step - n_grp) for step in range(1, n_grp)
    ]
    rows = [row] + [
        jnp.where(row + step < n_row, row + step, row + step - n_row) for step in range(1, n_row)
    ]
    blocks = {
        0: (grp, row),
        1: (jnp.where(row == n_row - 1, grps[1], grp), rows[1]),
        -1: (jnp.where(row == 0, grps[-1], grp), rows[-1]),
    }
    beside = tuple(
        jnp.where(half == 1, after, before) for before, after in zip(blocks[-1], blocks[1])
    )
    far_first = (4, 3, 5, 2, 6, 1, 7, 0)

    def device(block, plane, side):
        return block + (plane * 2 + side,)

    barrier = pltpu.get_barrier_semaphore()

    def say(target):
        pl.semaphore_signal(barrier, inc=1, device_id=target, device_id_type=MESH)

    for off in far_first:
        for step in range(n_grp):
            for side in (0, 1):
                if off or step:
                    say((grps[step], rows[off], 2 * pln + side))
    say(device(blocks[0], pln, other))
    for step in (-1, 1):
        @pl.when(there(pln + step))
        def _(step=step):
            for side in (0, 1):
                say(device(blocks[0], pln + step, side))
                say(device(beside, pln + step, side))

    @pl.when(there(pln - 2))
    def _():
        say(device(blocks[0], pln - 2, 1))

    @pl.when(there(pln + 2))
    def _():
        say(device(blocks[0], pln + 2, 0))

    x_copy = pltpu.make_async_copy(x_hbm, x_mat, weight_sem.at[0])
    z_copy = pltpu.make_async_copy(z_hbm, z_mat, weight_sem.at[1])
    x_copy.start()
    z_copy.start()

    for group in range(4):
        for comp in range(3):
            for chunk in range(8):
                spread[comp, pl.ds(group * 64 + chunk, 8, stride=8), :] = velocity_ref[
                    comp, 0, group * 8:(group + 1) * 8, chunk * 128:(chunk + 1) * 128
                ]

    def encode_cells(step, carry):
        for cell in range(4):
            start = pl.multiple_of((step * 4 + cell) * 8, 8)
            for comp in range(3):
                coded[step * 4 + cell, comp] = encode(spread[comp, pl.ds(start, 8), :])
        return carry

    lax.fori_loop(0, 2 * HALF // 4, encode_cells, 0)
    own_profile = jnp.full((8, 128), profile_ref[0], jnp.int32)
    for comp in range(3):
        coded[2 * HALF, comp] = own_profile.astype(jnp.int16)

    partners = 2 * n_blk - 1
    for step, count in ((toward, 4), (-toward, 4), (2 * toward, 2)):
        partners = partners + jnp.where(there(pln + step), count, 0)
    pl.semaphore_wait(barrier, partners)

    def give(source, count, cell, part, line, kind, target):
        pltpu.make_async_remote_copy(
            src_ref=coded.at[pl.ds(source, count)],
            dst_ref=gathered.at[pl.ds(line * WIDE + cell, count)],
            send_sem=gather_send.at[kind], recv_sem=gather_recv.at[part, line],
            device_id=target, device_id_type=MESH,
        ).start()

    pltpu.make_async_remote_copy(
        src_ref=coded.at[pl.ds(2 * HALF, 1)], dst_ref=gathered.at[pl.ds(CELLS, 1)],
        send_sem=gather_send.at[4], recv_sem=profile_sem,
        device_id=device(blocks[0], pln, other), device_id_type=MESH,
    ).start()

    own_line = DEPTH + half
    lines = (own_line, 5 - 3 * half, 1 + 5 * half, 7 - 7 * half)
    steps = (0, toward, -toward, 2 * toward)
    for part in range(2):
        for d in range(4):
            def main(side, d=d, part=part):
                target = device(blocks[0], pln + steps[d], side)
                if part == 0 and side == 0:
                    give(0, 11 - d, DEPTH, part, lines[d], d, target)
                elif part == 0:
                    give(13 + d, 14 - 2 * d, d, part, lines[d], d, target)
                elif side == 0:
                    give(11 - d, PART, 14 - d, part, lines[d], d, target)
                else:
                    give(27 - d, 5 + d, 14 - d, part, lines[d], d, target)

            def strip(d=d, part=part):
                if d == 3:
                    return
                if part == 0:
                    give(29 + d, 3 - d, d, part, lines[d], d, device(blocks[1], pln + steps[d], 0))
                else:
                    give(0, 3 - d, DEPTH + HALF, part, lines[d], d, device(blocks[-1], pln + steps[d], 1))

            if d == 0:
                for side in (0, 1):
                    pl.when(half != side)(functools.partial(main, side))
                strip()
            else:
                @pl.when(there(pln + steps[d]))
                def _(main=main, strip=strip):
                    main(0)
                    main(1)
                    strip()

    present = [
        (2 * pln - DEPTH + line >= 0) & (2 * pln - DEPTH + line < n_col) for line in range(ROWS)
    ]
    inside = [jnp.where(known, 1.0, 0.0).astype(F32) for known in present]

    for line in (0, 1, 2, 5, 6, 7):
        @pl.when(jnp.logical_not(present[line]))
        def _(line=line):
            def clear(cell, carry):
                for comp in range(3):
                    wide[line * WIDE + cell, comp] = jnp.zeros((8, 128), F32)
                return carry

            lax.fori_loop(0, WIDE, clear, 0)

    def keep(cell, carry):
        start = pl.multiple_of(((HALF - DEPTH) * half + cell) * 8, 8)
        for comp in range(3):
            wide[own_line * WIDE + DEPTH * other + cell, comp] = spread[comp, pl.ds(start, 8), :]
        return carry

    lax.fori_loop(0, HALF + DEPTH, keep, 0)

    length = 2 * n_blk * HALF

    def reorder(step, carry):
        start = pl.multiple_of(step * 128, 128)
        place = lax.broadcasted_iota(jnp.int32, (128, length), 0) + start
        within = lax.rem(place, length // 2)
        cell = (within // PART) * HALF + (place // (length // 2)) * PART + lax.rem(within, PART)
        hit = cell == lax.broadcasted_iota(jnp.int32, (128, length), 1)
        order[pl.ds(start, 128), :] = jnp.where(hit, 1.0, 0.0).astype(BF16)
        return carry

    lax.fori_loop(0, length // 128, reorder, 0)
    z_copy.wait()

    def turn_z(step, carry):
        start = pl.multiple_of(step * 256, 256)
        z_turned[:, pl.ds(start, 256)] = lax.dot_general(
            order[...], z_mat[pl.ds(start, 256), :], (((1,), (1,)), ((), ())),
            preferred_element_type=F32,
        ).astype(BF16)
        return carry

    lax.fori_loop(0, 4, turn_z, 0)

    def arrive(part, line, low, count):
        pltpu.make_async_copy(
            gathered.at[pl.ds(0, count)], gathered.at[pl.ds(0, count)], gather_recv.at[part, line]
        ).wait()
        per = count // 2 if count % 2 == 0 else count

        def some(step, carry):
            for cell in range(per):
                here = line * WIDE + low + step * per + cell
                for comp in range(3):
                    wide[here, comp] = decode(gathered[here, comp])
            return carry

        lax.fori_loop(0, count // per, some, 0)

    lane = lax.broadcasted_iota(jnp.int32, (8, 128), 1)
    last_lane, first_lane = lane == 127, lane == 0

    def advance(source, scale, old, here):
        weight, advect = 0.2 * scale, 0.125 * scale
        center = [source[here, comp] for comp in range(3)]
        pairs = []
        for comp in range(3):
            scaled = center[comp] * advect
            pairs.append((weight - scaled, weight + scaled))
        results = []
        for comp in range(3):
            value = center[comp]
            ahead = pltpu.roll(value, 127, 1)
            ahead = jnp.where(last_lane, pltpu.roll(ahead, 7, 0), ahead)
            behind = pltpu.roll(value, 1, 1)
            behind = jnp.where(first_lane, pltpu.roll(behind, 1, 0), behind)
            total = (pairs[0][0] * ahead + pairs[0][1] * behind) + (
                pairs[1][0] * source[here + WIDE, comp] + pairs[1][1] * source[here - WIDE, comp]
            )
            total = total + (
                pairs[2][0] * source[here + 1, comp] + pairs[2][1] * source[here - 1, comp]
            )
            total = total - weight * value
            if old:
                total = total + old * wide[here, comp]
            results.append(total)
        return results

    def sweep(number, part, d):
        source = (wide, first, second)[number - 1]
        scale, old = ((1.0, None), (0.25, 0.75), (2.0 / 3.0, 1.0 / 3.0))[number - 1]
        low, high = ((d + number, 14 - d - number), (14 - d - number, 22 - d - number))[part]

        per = {12: 6, 10: 5, 8: 8}[high - low]

        def some(step, carry):
            done = []
            for line in (DEPTH - d, DEPTH + 1 + d):
                for cell in range(per):
                    place = low + per * step + cell
                    done.append((line, place, advance(source, scale, old, line * WIDE + place)))
            for line, place, results in done:
                for comp in range(3):
                    value = results[comp]
                    if number == 3:
                        start = ((part * 2 + line - DEPTH) * PART + place - low) * 8
                        advanced[comp, pl.ds(pl.multiple_of(start, 8), 8), :] = value
                        continue
                    if d:
                        value = value * inside[line]
                    (first, second)[number - 1][line * WIDE + place, comp] = value
            return carry

        lax.fori_loop(0, (high - low) // per, some, 0)

    wide_lane = lax.broadcasted_iota(jnp.int32, (2 * PART, 128), 1)
    quarter = wide_lane // 32
    small_quarter = lane // 32
    spot = 2 * blk + half

    def pass_part(part, one, zero):
        for chunk in range(8):
            comps = [
                advanced[comp, pl.ds(part * 128 + chunk, 2 * PART, stride=8), :] for comp in range(3)
            ]
            for number, factors in enumerate(FIELD_FACTORS):
                field = functools.reduce(lambda a, b: a * b, [comps[f] for f in factors])
                lines = slice(number * 2 * PART, (number + 1) * 2 * PART)
                fields[lines, chunk * 128:(chunk + 1) * 128] = (field * zero).astype(BF16)
                fields[lines, 1024 + chunk * 128:1024 + (chunk + 1) * 128] = (field * one).astype(BF16)
        send_ref = (send_first, send_second)[part]
        recv_ref = (recv_first, recv_second)[part]

        def outputs(step, carry):
            dest_grp = lax.rem(grp + 1 + step, n_grp)
            start = pl.multiple_of(dest_grp * n_row * 32, 256)
            contract = (((1,), (1,)), ((), ()))
            passed = lax.dot_general(
                fields[:, 0:1024], x_mat[0, pl.ds(start, 256), :], contract,
                preferred_element_type=F32,
            ) + lax.dot_general(
                fields[:, 1024:2048], x_mat[1, pl.ds(start, 256), :], contract,
                preferred_element_type=F32,
            )
            if part == 0:
                last_low[:, pl.ds(start, 256)] = passed[128:144]
            else:
                lows = last_low[:, pl.ds(start, 256)]
            for tile in range(2):
                lanes = slice(tile * 128, (tile + 1) * 128)
                for four in range(2):
                    turned = []
                    for k in range(4):
                        piece = passed[(four * 4 + k) * 16:(four * 4 + k + 1) * 16, lanes]
                        turned.append(pltpu.roll(piece, 32 * k, 1) if k else piece)
                    for place in range(4):
                        mixed = turned[3]
                        for k in range(3):
                            mixed = jnp.where(quarter == (place + k) % 4, turned[k], mixed)
                        dest = dest_grp * n_row + tile * 4 + place
                        send_ref[dest, four] = mixed[0:PART].astype(BF16)
                        send_ref[n_blk + dest, four] = mixed[PART:2 * PART].astype(BF16)
                if part == 1:
                    for line in range(2):
                        band = slice(line * PART, (line + 1) * PART)
                        high = pltpu.roll(passed[128:144, lanes][band], 32, 1)
                        low = lows[band, lanes]
                        for place in range(4):
                            dest = dest_grp * n_row + tile * 4 + place
                            send_ref[line * n_blk + dest, 2] = jnp.where(
                                small_quarter == place, low, high
                            ).astype(BF16)
            for off in far_first:
                dest_row = rows[off]
                dest = dest_grp * n_row + dest_row
                for line in range(2):
                    target = (dest_grp, dest_row, 2 * pln + line)

                    def send(line=line, target=target, dest=dest):
                        pltpu.make_async_remote_copy(
                            src_ref=send_ref.at[line * n_blk + dest], dst_ref=recv_ref.at[spot],
                            send_sem=pass_send.at[part], recv_sem=pass_recv.at[part],
                            device_id=target, device_id_type=MESH,
                        ).start()

                    if off:
                        send()
                    else:
                        pl.when((dest != blk) | (half != line))(send)
            return carry

        lax.fori_loop(0, n_grp, outputs, 0)
        stay = pltpu.make_async_copy(
            send_ref.at[half * n_blk + blk], recv_ref.at[spot], local_sem.at[part]
        )
        stay.start()
        return stay

    stays = []
    for part in range(2):
        for d in range(4):
            if d == 0:
                arrive(part, 4 - half, (0, 14)[part], (14, PART)[part])
                pl.when(half == part)(
                    functools.partial(arrive, part, own_line, (0, DEPTH + HALF)[part], DEPTH)
                )
                continue
            for line in (DEPTH - d, DEPTH + 1 + d):
                pl.when(present[line])(
                    functools.partial(arrive, part, line, (d, 14 - d)[part], (14 - 2 * d, PART)[part])
                )
            for number in range(1, d + 1):
                sweep(number, part, d - number)
        if part == 0:
            pltpu.make_async_copy(
                gathered.at[pl.ds(0, 1)], gathered.at[pl.ds(0, 1)], profile_sem
            ).wait()
            pair_profile = gathered[CELLS, 0].astype(jnp.int32)
            even = jnp.where(half == 0, own_profile, pair_profile).astype(F32)
            odd = jnp.where(half == 0, pair_profile, own_profile).astype(F32)
            one = jnp.concatenate([even, odd], axis=0)
            x_copy.wait()
        stays.append(pass_part(part, one, 1.0 - one))

    contract = (((0,), (0,)), ((), ()))
    many = 2 * n_blk - 1
    middle = length // 2

    def z_filter(cells, rows):
        return lax.dot_general(
            cells.reshape(cells.shape[0] * PART, 128).astype(BF16), z_turned[rows, :], contract,
            preferred_element_type=F32,
        )

    for part, ref in ((0, recv_first), (1, recv_second)):
        stays[part].wait()
        pltpu.make_async_copy(
            ref.at[pl.ds(0, many)], ref.at[pl.ds(0, many)], pass_recv.at[part]
        ).wait()
        cells = slice(part * middle, (part + 1) * middle)
        for four in range(2):
            filtered_part = z_filter(ref[:, four].astype(F32), cells)
            lines = slice(four * 128, (four + 1) * 128)
            if part == 0:
                z_pass[lines, :] = filtered_part
            else:
                z_pass[lines, :] = z_pass[lines, :] + filtered_part
    low = recv_second[:, 2].astype(F32)
    high = pltpu.roll(low.reshape(2 * n_blk * PART, 128), 96, 1).reshape(2 * n_blk, PART, 128)
    z_pass[256:384, :] = z_filter(jnp.concatenate([low, high], axis=0), slice(0, length))

    turn = lax.rem(row, 4)

    def filtered(number):
        start = (number // 4) * 128 + lax.rem(turn + number % 4, 4) * 32
        return z_pass[pl.ds(pl.multiple_of(start, 32), 32), :]

    linear = [filtered(number) for number in range(3)]
    for number, (left, right) in enumerate(PRODUCT_PAIRS):
        direct_ref[number, 0] = filtered(3 + number)
        product_ref[number, 0] = linear[left] * linear[right]

    def sent(sem, count):
        pltpu.make_async_copy(gathered.at[pl.ds(0, count)], gathered.at[pl.ds(0, count)], sem).wait()

    sent(gather_send.at[4], 1)
    sent(gather_send.at[0], 25)
    for d, count in ((1, 40), (2, 36), (3, 32)):
        pl.when(there(pln + steps[d]))(functools.partial(sent, gather_send.at[d], count))
    for part, ref in ((0, send_first), (1, send_second)):
        pltpu.make_async_copy(
            ref.at[pl.ds(0, many)], ref.at[pl.ds(0, many)], pass_send.at[part]
        ).wait()


def solution(mesh):
    sizes = (mesh.shape["grp"], mesh.shape["row"], mesh.shape["col"])
    n_blk = sizes[0] * sizes[1]
    tile = (8, 128)

    def body(velocity, profile, x_filters, z_filter):
        vmem = pl.BlockSpec(memory_space=pltpu.VMEM)
        result = pltpu.VMEM((6, 1, 32, 1024), F32)
        direct, product = pl.pallas_call(
            functools.partial(kernel, sizes),
            out_shape=(result, result),
            in_specs=[
                pl.BlockSpec(memory_space=pltpu.SMEM),
                vmem,
                pl.BlockSpec(memory_space=pl.ANY),
                pl.BlockSpec(memory_space=pl.ANY),
            ],
            out_specs=(vmem, vmem),
            scratch_shapes=[
                pltpu.VMEM((3, 256, 128), F32),
                pltpu.VMEM((2 * HALF + 1, 3) + tile, jnp.int16),
                pltpu.VMEM((CELLS + 1, 3) + tile, jnp.int16),
                pltpu.VMEM((CELLS, 3) + tile, F32),
                pltpu.VMEM((CELLS, 3) + tile, F32),
                pltpu.VMEM((CELLS, 3) + tile, F32),
                pltpu.VMEM((3, 256, 128), F32),
                pltpu.VMEM((9 * 2 * PART, 2048), BF16),
                pltpu.VMEM((2 * PART, 1024), F32),
                pltpu.VMEM((2, 1024, 1024), BF16),
                pltpu.VMEM((1024, 1024), BF16),
                pltpu.VMEM((2 * n_blk, 2) + tile, BF16),
                pltpu.VMEM((2 * n_blk, 3) + tile, BF16),
                pltpu.VMEM((2 * n_blk, 2) + tile, BF16),
                pltpu.VMEM((2 * n_blk, 3) + tile, BF16),
                pltpu.VMEM((384, 1024), F32),
                pltpu.VMEM((1024, 1024), BF16),
                pltpu.VMEM((1024, 1024), BF16),
                pltpu.SemaphoreType.DMA((2,)),
                pltpu.SemaphoreType.DMA((5,)),
                pltpu.SemaphoreType.DMA((2, ROWS)),
                pltpu.SemaphoreType.DMA,
                pltpu.SemaphoreType.DMA((2,)),
                pltpu.SemaphoreType.DMA((2,)),
                pltpu.SemaphoreType.DMA((2,)),
            ],
            compiler_params=pltpu.CompilerParams(
                collective_id=0, has_side_effects=True, vmem_limit_bytes=60000 * 1024
            ),
            name="subgrid",
        )(profile, velocity, x_filters, z_filter)
        return direct - product

    placed = (P(None, "col", ("grp", "row"), None), P("col"), P(), P())
    return jax.shard_map(
        body,
        mesh=mesh,
        in_specs=placed,
        out_specs=P(None, "col", ("grp", "row"), None),
        check_vma=False,
    )
```
